128 devices in a mesh: node: 8 (over y, core), local: 16 (over x, z).
Axes of the slice: x: 4, y: 4, z: 4, core: 2. Of those that a mesh axis runs over, the one named last changes fastest.
Arguments:
- tokens: bfloat16 [16384, 3584], P(('node', 'local')), may hold values from -3 to 3
- act_scale: float32 [16384, 28], P(('node', 'local')), may hold values from 0.25 to 4, as said below
- routes: int32 [16384, 8], P(('node', 'local')), may hold values from 0 to 127, all different within a row; in each aligned block of 128 rows (0 to 127, 128 to 255, ...) at most 10 rows name the same one
- combine: float32 [16384, 8], P(('node', 'local')), may hold values from 0.1 to 0.6
- w_gate: bfloat16 [128, 3584, 1024], P(('node', 'local')), may hold values from -0.046875 to 0.046875
- gate_scale: float32 [128, 28, 8], P(('node', 'local')), may hold values from 0.25 to 4, as said below
- w_up: bfloat16 [128, 3584, 1024], P(('node', 'local')), may hold values from -0.046875 to 0.046875
- up_scale: float32 [128, 28, 8], P(('node', 'local')), may hold values from 0.25 to 4, as said below
- w_down: bfloat16 [128, 1024, 3584], P(('node', 'local')), may hold values from -0.09375 to 0.09375
- down_scale: float32 [128, 8, 28], P(('node', 'local')), may hold values from 0.25 to 4, as said below
Outputs:
- combined: bfloat16 [16384, 3584], P(('node', 'local'))
The draws below stay inside these ranges and needn't reach their ends.
Inputs may be any that keep to these rules, and one draw needn't show every extreme that they name: `routes`: each token names 8 different experts. Among the 128 tokens of one device (aligned blocks), no expert is named more than 10 times, and in some blocks one expert is named exactly 10 times. `act_scale`: every entry is a power of two. `gate_scale`: every entry is a power of two. `up_scale`: every entry is a power of two. `down_scale`: every entry is a power of two.
All inputs are finite; a program needn't handle non-finite values.
Results may differ from the reference program's by a relative error of at most 0.0058.
Values may be sent and summed in bfloat16 or wider, within the bound.
No kernel may reach another device: no remote copies, remote signals or barrier semaphores. Data moves between devices by JAX's collectives and lax.ppermute only.
A program may use at most 192 MiB of HBM per device.

```python
import math
import jax
import jax.numpy as jnp
import numpy as np
from jax import lax

D = 3584
FF = 1024
TOP = 8
BLOCK = 128
TOK_DEV = 128
EXPERTS = 128
CAP = 10
TOKENS = 16384


def power_table(key, shape):
    exponent = jax.random.randint(key, shape, -2, 3)
    return jnp.exp2(exponent.astype(jnp.float32))


def draw_act_scale(key, part):
    return power_table(jax.random.fold_in(key, 11), (TOKENS, D // BLOCK))


def draw_gate_scale(key, part):
    return power_table(jax.random.fold_in(key, 23), (EXPERTS, D // BLOCK, FF // BLOCK))


def draw_up_scale(key, part):
    return power_table(jax.random.fold_in(key, 37), (EXPERTS, D // BLOCK, FF // BLOCK))


def draw_down_scale(key, part):
    return power_table(jax.random.fold_in(key, 41), (EXPERTS, FF // BLOCK, D // BLOCK))


def shard_levels(own_key, extent, pieces, low, top_value):
    level, own = 1.0, jax.random.fold_in(own_key, 6)
    for axis_at, blocks in pieces:
        steps = jnp.exp(jax.random.uniform(jax.random.fold_in(own, axis_at), (blocks,), jnp.float32, low / len(pieces), top_value / len(pieces)))
        level = level * jnp.repeat(steps, extent[axis_at] // blocks).reshape([-1 if axis == axis_at else 1 for axis in range(len(extent))])
    return level


def assign_block(stream_key, own, number, rows, amount, top, reach, lean):
    order = jax.random.permutation(stream_key, amount)
    packed, common = load_shares(amount, rows * top, reach, lean, True), load_shares(amount, rows * top, reach, lean, False)
    places = jnp.arange(amount)

    def named(tallies, offset_by):
        used = int((tallies > 0).sum())
        fixed = max(1, used // 4)
        passed = fixed + (places - fixed + offset_by * (used - fixed)) % max(1, amount - fixed)
        return jnp.zeros((amount,), jnp.int32).at[order[jnp.where(places < fixed, places, passed)]].set(jnp.asarray(tallies, jnp.int32))

    tallies = jnp.where(number % 4 == 0, named(packed, number // 4), named(common, number - number // 4 - 1))
    mixed = jax.random.permutation(jax.random.fold_in(own, 3), amount)
    donor, receiver = mixed[0:amount // 2 * 2:2], mixed[1:amount // 2 * 2:2]
    slack = jnp.minimum(tallies[donor] - 1, reach - tallies[receiver]) // 2
    slack = jnp.where((donor == order[0]) | (receiver == order[0]) | (tallies[receiver] == 0), 0, jnp.maximum(slack, 0))
    passed = jax.random.randint(jax.random.fold_in(own, 4), (amount // 2,), 0, 1 << 20) % (slack + 1)
    tallies = tallies.at[donor].add(-passed).at[receiver].add(passed)
    labels = jnp.searchsorted(jnp.cumsum(tallies), jnp.arange(rows * top), side="right").astype(jnp.int32)
    grid = labels.reshape(top, rows).T
    grid = grid[jax.random.permutation(jax.random.fold_in(own, 1), rows)]
    offset_by = jax.random.randint(jax.random.fold_in(own, 2), (rows, 1), 0, top)
    return jnp.take_along_axis(grid, (jnp.arange(top)[None, :] + offset_by) % top, axis=1)


def load_shares(count, total, limit, slope, full):
    loads = [(1 << 20) // math.isqrt(standing ** slope) + 1 for standing in range(1, count + 1)]
    largest = limit if full else min(limit, max(-(-total // count), total * loads[0] // sum(loads)))
    least = 1 if total - largest >= count - 1 else 0
    counts, rest = [largest] + [least] * (count - 1), total - largest - least * (count - 1)
    while rest > 0:
        free = [i for i in range(1, count) if counts[i] < largest] or [i for i in range(1, count) if counts[i] < limit]
        mass, remaining = sum([loads[i] for i in free]), rest
        for i in free:
            extra = min(limit - counts[i], max(1, remaining * loads[i] // mass), rest)
            counts[i] = counts[i] + extra
            rest = rest - extra
    return np.array(counts)


def scatter_about(own_key, extent, scale, reach, shards=(), held_as=jnp.bfloat16):
    factor_of = shard_levels(own_key, extent, shards, -0.22, 0.18) if shards else 1.0
    entries = jax.random.normal(own_key, extent, jnp.float32) * scale * factor_of
    return jnp.minimum(jnp.maximum(entries, -reach), reach).astype(held_as)


def setup_inputs(seed: int = 0) -> dict:
    streams_of = jax.random.split(jax.random.key(seed), 11)
    tokens = scatter_about(streams_of[0], (TOKENS, D), 0.5, 3.0, ((0, 128),))
    act_scale = draw_act_scale(jax.random.fold_in(streams_of[10], 71), 0)
    routes_keys = jax.random.split(jax.random.fold_in(streams_of[2], 1), TOKENS // TOK_DEV)
    routes_turns = jax.random.permutation(jax.random.fold_in(streams_of[2], 3), TOKENS // TOK_DEV)
    routes = jax.vmap(lambda own, number: assign_block(jax.random.fold_in(streams_of[2], 2), own, number, TOK_DEV, EXPERTS, TOP, CAP, 1))(routes_keys, routes_turns).reshape((TOKENS, TOP))
    combine = jnp.clip(0.1 + 0.5 * jax.random.uniform(streams_of[3], (TOKENS, TOP), jnp.float32) ** shard_levels(streams_of[3], (TOKENS, TOP), ((0, 128),), -0.2, 0.2), 0.1, 0.6)
    w_gate = scatter_about(streams_of[4], (EXPERTS, D, FF), (4 * D) ** -0.5, 0.046875, ((0, 128),))
    gate_scale = draw_gate_scale(jax.random.fold_in(streams_of[10], 71), 0)
    w_up = scatter_about(streams_of[6], (EXPERTS, D, FF), (4 * D) ** -0.5, 0.046875, ((0, 128),))
    up_scale = draw_up_scale(jax.random.fold_in(streams_of[10], 71), 0)
    w_down = scatter_about(streams_of[8], (EXPERTS, FF, D), (4 * FF) ** -0.5, 0.09375, ((0, 128),))
    down_scale = draw_down_scale(jax.random.fold_in(streams_of[10], 71), 0)
    return dict(tokens=tokens, act_scale=act_scale, routes=routes, combine=combine, w_gate=w_gate, gate_scale=gate_scale, w_up=w_up, up_scale=up_scale, w_down=w_down, down_scale=down_scale)


def expand_scale(scale_table):
    return jnp.repeat(jnp.repeat(scale_table, BLOCK, axis=0), BLOCK, axis=1)


def dequantize(weight, scale_table):
    return (weight.astype(jnp.float32) * expand_scale(scale_table)).astype(jnp.bfloat16)


def reference(tokens, act_scale, routes, combine, w_gate, gate_scale, w_up, up_scale, w_down, down_scale):
    inputs = (tokens.astype(jnp.float32) * jnp.repeat(act_scale, BLOCK, axis=1)).astype(jnp.bfloat16)
    flat_routes = routes.reshape(-1).astype(jnp.int32)
    flat_weight = combine.reshape(-1)
    owner_row = (jnp.arange(TOKENS * TOP) // TOP).astype(jnp.int32)
    slot_total = EXPERTS * CAP

    def visit_expert(expert_id, running):
        hits = flat_routes == expert_id
        hit_count = jnp.sum(hits.astype(jnp.int32))
        picked_pairs = jnp.nonzero(hits, size=slot_total, fill_value=0)[0].astype(jnp.int32)
        present = jnp.arange(slot_total).astype(jnp.int32) < hit_count
        target_rows = owner_row[picked_pairs]
        row_block = inputs[target_rows]
        gate_full = dequantize(lax.dynamic_index_in_dim(w_gate, expert_id, 0, keepdims=False),
                               lax.dynamic_index_in_dim(gate_scale, expert_id, 0, keepdims=False))
        up_full = dequantize(lax.dynamic_index_in_dim(w_up, expert_id, 0, keepdims=False),
                             lax.dynamic_index_in_dim(up_scale, expert_id, 0, keepdims=False))
        down_full = dequantize(lax.dynamic_index_in_dim(w_down, expert_id, 0, keepdims=False),
                               lax.dynamic_index_in_dim(down_scale, expert_id, 0, keepdims=False))
        gate_value = jnp.dot(row_block, gate_full, preferred_element_type=jnp.float32)
        up_value = jnp.dot(row_block, up_full, preferred_element_type=jnp.float32)
        hidden = (jax.nn.silu(gate_value) * up_value).astype(jnp.bfloat16)
        expert_out = jnp.dot(hidden, down_full, preferred_element_type=jnp.float32).astype(jnp.bfloat16)
        pair_weight = jnp.where(present, flat_weight[picked_pairs], jnp.zeros_like(flat_weight[picked_pairs]))
        return running.at[target_rows].add(pair_weight[:, None] * expert_out.astype(jnp.float32))

    start = jnp.zeros((TOKENS, D), jnp.float32)
    running = lax.fori_loop(0, EXPERTS, visit_expert, start)
    return running.astype(jnp.bfloat16)
```

```python
import jax
import jax.numpy as jnp
from jax import lax
from jax.sharding import PartitionSpec as P

AXES = ("node", "local")


def dequantize(weight, scale_table, scale_block):
    row_count, col_count = weight.shape
    scale_bf = scale_table.astype(jnp.bfloat16)
    shaped = weight.reshape(
        row_count // scale_block, scale_block, col_count // scale_block, scale_block
    )
    return (shaped * scale_bf[:, None, :, None]).reshape(row_count, col_count)


def exchange(block):
    return lax.all_to_all(block, AXES, split_axis=0, concat_axis=0, tiled=True)


def groups_of(slots):
    at, groups = slots[0], []
    for size in (8, 4, 2):
        while slots[1] - at >= size:
            groups.append((at, size))
            at += size
    return groups


def pack(onehot, inputs, slots):
    experts, _, rows = onehot.shape
    width = inputs.shape[1]
    parts = []
    for at, size in groups_of(slots):
        cuts = 8 // size
        piece = width // cuts
        stacked = jnp.concatenate(
            [inputs[:, c * piece : (c + 1) * piece] for c in range(cuts)], axis=0
        )
        picks = onehot[:, at : at + size, :]
        table = jnp.stack(
            [
                jnp.concatenate(
                    [picks if c == d else jnp.zeros_like(picks) for d in range(cuts)], axis=2
                )
                for c in range(cuts)
            ],
            axis=1,
        ).reshape(experts * 8, cuts * rows)
        parts.append(
            jnp.dot(table, stacked, preferred_element_type=jnp.float32)
            .astype(jnp.bfloat16)
            .reshape(experts, 8, piece)
        )
    return jnp.concatenate(parts, axis=2)


def unfold(block, slots, width):
    experts = block.shape[0]
    rows, lane = [], 0
    for at, size in groups_of(slots):
        cuts = 8 // size
        piece = width // cuts
        rows.append(
            block[:, :, lane : lane + piece]
            .reshape(experts, cuts, size, piece)
            .transpose(0, 2, 1, 3)
            .reshape(experts * size, width)
        )
        lane += piece
    return jnp.concatenate(rows, axis=0)


def fold(rows, slots, experts):
    width = rows.shape[1]
    parts, first = [], 0
    for at, size in groups_of(slots):
        cuts = 8 // size
        piece = width // cuts
        parts.append(
            rows[first : first + experts * size]
            .reshape(experts, size, cuts, piece)
            .transpose(0, 2, 1, 3)
            .reshape(experts, 8, piece)
        )
        first += experts * size
    return jnp.concatenate(parts, axis=2)


def merge(block, weights, slots, width):
    experts = block.shape[0]
    tokens = weights[0].shape[0]
    total, lane = 0.0, 0
    for at, size in groups_of(slots):
        cuts = 8 // size
        piece = width // cuts
        rows = block[:, :, lane : lane + piece].reshape(experts * 8, piece)
        lane += piece
        tables = []
        for c in range(cuts):
            for term in weights:
                own = term[:, :, at : at + size]
                tables.append(
                    jnp.concatenate(
                        [own if c == d else jnp.zeros_like(own) for d in range(cuts)], axis=2
                    ).reshape(tokens, experts * 8)
                )
        sums = jnp.dot(
            jnp.concatenate(tables, axis=0), rows, preferred_element_type=jnp.float32
        ).reshape(cuts, len(weights), tokens, piece)
        total = total + jnp.concatenate([sums[c].sum(axis=0) for c in range(cuts)], axis=1)
    return total


def expert_forward(row_block, gate_full, up_full, down_full):
    gate_value = jnp.dot(row_block, gate_full, preferred_element_type=jnp.float32)
    up_value = jnp.dot(row_block, up_full, preferred_element_type=jnp.float32)
    hidden = (jax.nn.silu(gate_value) * up_value).astype(jnp.bfloat16)
    return jnp.dot(hidden, down_full, preferred_element_type=jnp.float32).astype(jnp.bfloat16)


def local(
    tokens, act_scale, routes, combine, w_gate, gate_scale, w_up, up_scale, w_down, down_scale
):
    tok_rows, width = tokens.shape
    route_count = routes.shape[1]
    scale_block = width // act_scale.shape[1]
    experts = lax.axis_size("node") * lax.axis_size("local")
    capacity = 5 * tok_rows * route_count // (4 * experts)
    first = 6
    chunks = ((0, first), (first, capacity))
    inputs = (
        tokens.reshape(tok_rows, -1, scale_block) * act_scale.astype(jnp.bfloat16)[:, :, None]
    ).reshape(tok_rows, width)

    names = routes[:, :, None] == jnp.arange(experts, dtype=jnp.int32)[None, None, :]
    named = jnp.any(names, axis=1)
    weight = jnp.sum(jnp.where(names, combine[:, :, None], 0.0), axis=1)
    order = jnp.arange(tok_rows, dtype=jnp.int32)
    earlier = (order[None, :] < order[:, None]).astype(jnp.bfloat16)
    rank = jnp.dot(earlier, named.astype(jnp.bfloat16), preferred_element_type=jnp.float32)
    rank = jnp.where(named, rank, -1.0).astype(jnp.int32)
    slot = jnp.arange(capacity, dtype=jnp.int32)
    onehot = (rank.T[:, None, :] == slot[None, :, None]).astype(jnp.bfloat16)
    spread = jnp.where(rank[:, :, None] == slot[None, None, :], weight[:, :, None], 0.0)
    high = spread.astype(jnp.bfloat16)
    low = (spread - high.astype(jnp.float32)).astype(jnp.bfloat16)

    gate_full = dequantize(w_gate[0], gate_scale[0], scale_block)
    up_full = dequantize(w_up[0], up_scale[0], scale_block)
    down_full = dequantize(w_down[0], down_scale[0], scale_block)

    arrived = [exchange(pack(onehot, inputs, chunk)) for chunk in chunks]
    outcome = [
        fold(
            expert_forward(unfold(block, chunk, width), gate_full, up_full, down_full),
            chunk,
            experts,
        )
        for block, chunk in zip(arrived, chunks)
    ]
    returned = [exchange(block) for block in outcome]
    total = merge(returned[0], (high, low), chunks[0], width)
    total = total + merge(returned[1], (high, low), chunks[1], width)
    return total.astype(jnp.bfloat16)


def solution(mesh):
    placed = (P(AXES, None),) * 4 + (P(AXES, None, None),) * 6
    return jax.shard_map(
        local, mesh=mesh, in_specs=placed, out_specs=P(AXES, None), check_vma=False
    )
```

```python
import functools

import jax
import jax.numpy as jnp
from jax import lax
from jax.experimental import pallas as pl
from jax.experimental.pallas import tpu as pltpu
from jax.sharding import PartitionSpec as P


AXES = ("node", "local")
BLOCK = 128
PART = 4
FIRST = 6
BF = jnp.bfloat16
F32 = jnp.float32


def groups_of(first, last):
    groups = []
    for size in (8, 4, 2):
        while last - first >= size:
            groups.append((first, size))
            first += size
    return groups


def ranks(names):
    count, rows = names.shape
    expert = lax.broadcasted_iota(jnp.int32, (rows, rows), 0)
    named = jnp.zeros((rows, rows), F32)
    for k in range(count):
        named = named + jnp.where(names[k : k + 1, :] == expert, 1.0, 0.0)
    later = lax.broadcasted_iota(jnp.int32, (rows, rows), 0) < lax.broadcasted_iota(
        jnp.int32, (rows, rows), 1
    )
    before = jnp.dot(
        named.astype(BF), jnp.where(later, 1.0, 0.0).astype(BF), preferred_element_type=F32
    )
    return jnp.where(named > 0.5, before, -1.0)


def eightfold(table):
    rows, cols = table.shape
    return jnp.broadcast_to(table[:, None, :], (rows, 8, cols)).reshape(rows * 8, cols)


def places(shape, size):
    row = lax.broadcasted_iota(jnp.int32, shape, 0)
    return (row & (size - 1)).astype(F32), (row & 7) >> (size.bit_length() - 1)


def turn(size, back):
    shape = (256, 256)
    out = lax.broadcasted_iota(jnp.int32, shape, 1 if back else 0)
    held = lax.broadcasted_iota(jnp.int32, shape, 0 if back else 1)
    low = size.bit_length() - 1
    piece = out >> (5 + low)
    source = (out >> low) & 31
    slot = out & (size - 1)
    return jnp.where(held == source * 8 + piece * size + slot, 1.0, 0.0).astype(BF)


def pack_kernel(groups, tokens_ref, scale_ref, names_ref, out_ref):
    _, width = tokens_ref.shape
    blocks = scale_ref.shape[0]
    lane = lax.broadcasted_iota(jnp.int32, (blocks, width), 1)
    spread = jnp.where(
        (lane >> 7) == lax.broadcasted_iota(jnp.int32, (blocks, width), 0), 1.0, 0.0
    ).astype(BF)
    scale = lax.dot_general(
        scale_ref[...].astype(BF), spread, (((0,), (0,)), ((), ())), preferred_element_type=F32
    )
    inputs = (tokens_ref[...].astype(F32) * scale).astype(BF)
    held = eightfold(ranks(names_ref[...]))
    start = 0
    for first, size in groups:
        cuts = 8 // size
        piece = width // cuts
        slot, cut = places(held.shape, size)
        match = held == slot + float(first)
        table = jnp.concatenate(
            [jnp.where(match & (cut == c), 1.0, 0.0).astype(BF) for c in range(cuts)], axis=1
        )
        stacked = jnp.concatenate(
            [inputs[:, c * piece : (c + 1) * piece] for c in range(cuts)], axis=0
        )
        out_ref[:, start : start + piece] = jnp.dot(
            table, stacked, preferred_element_type=F32
        ).astype(BF)
        start += piece


def pack(groups, tokens, scale, names):
    rows, width = tokens.shape
    wide = sum(width * size // 8 for _, size in groups)
    return pl.pallas_call(
        functools.partial(pack_kernel, groups),
        out_shape=jax.ShapeDtypeStruct((rows * 8, wide), BF),
        in_specs=[pl.BlockSpec(memory_space=pltpu.VMEM)] * 3,
        out_specs=pl.BlockSpec(memory_space=pltpu.VMEM),
        compiler_params=pltpu.CompilerParams(vmem_limit_bytes=40 << 20),
    )(tokens, scale, names)


def table_kernel(chunks, names_ref, weight_ref, *out_refs):
    names = names_ref[...]
    held = ranks(names)
    rows = held.shape[0]
    expert = lax.broadcasted_iota(jnp.int32, (rows, rows), 0)
    weight = jnp.zeros((rows, rows), F32)
    for k in range(names.shape[0]):
        weight = weight + jnp.where(names[k : k + 1, :] == expert, weight_ref[k : k + 1, :], 0.0)
    held, weight = eightfold(held), eightfold(weight)
    at = 0
    for groups in chunks:
        for first, size in groups:
            slot, cut = places(held.shape, size)
            match = held == slot + float(first)
            for c in range(8 // size):
                own = jnp.where(match & (cut == c), weight, 0.0).T
                high = own.astype(BF)
                low = (own - high.astype(F32)).astype(BF)
                out_refs[at][2 * c * rows : (2 * c + 1) * rows, :] = high
                out_refs[at][(2 * c + 1) * rows : (2 * c + 2) * rows, :] = low
            at += 1


def tables(chunks, names, weight):
    rows = names.shape[1]
    return pl.pallas_call(
        functools.partial(table_kernel, chunks),
        out_shape=[
            jax.ShapeDtypeStruct((2 * (8 // size) * rows, 8 * rows), BF)
            for groups in chunks
            for _, size in groups
        ],
        in_specs=[pl.BlockSpec(memory_space=pltpu.VMEM)] * 2,
        out_specs=[pl.BlockSpec(memory_space=pltpu.VMEM)] * sum(len(g) for g in chunks),
        compiler_params=pltpu.CompilerParams(vmem_limit_bytes=40 << 20),
    )(names, weight)


def dequantize_kernel(gate_ref, up_ref, down_ref, gs_ref, us_ref, ds_ref, g_ref, u_ref, d_ref):
    for weight_ref, scale_ref, out_ref in (
        (gate_ref, gs_ref, g_ref),
        (up_ref, us_ref, u_ref),
        (down_ref, ds_ref, d_ref),
    ):
        for k in range(weight_ref.shape[0] // BLOCK):
            part = slice(k * BLOCK, (k + 1) * BLOCK)
            out_ref[part, :] = (weight_ref[part, :].astype(F32) * scale_ref[k]).astype(BF)


def dequantize(gate, up, down, gate_scale, up_scale, down_scale):
    width, hidden = gate.shape
    steps = 7
    tall, wide = width // steps, width // steps
    across = lambda scale: jnp.repeat(scale, BLOCK, axis=1)[:, None, :]
    row_spec = pl.BlockSpec((tall, hidden), lambda i: (i, 0))
    col_spec = pl.BlockSpec((hidden, wide), lambda i: (0, i))
    row_scale = pl.BlockSpec((tall // BLOCK, 1, hidden), lambda i: (i, 0, 0))
    col_scale = pl.BlockSpec((hidden // BLOCK, 1, wide), lambda i: (0, 0, i))
    return pl.pallas_call(
        dequantize_kernel,
        grid=(steps,),
        out_shape=[jax.ShapeDtypeStruct(w.shape, BF) for w in (gate, up, down)],
        in_specs=[row_spec, row_spec, col_spec, row_scale, row_scale, col_scale],
        out_specs=[row_spec, row_spec, col_spec],
        compiler_params=pltpu.CompilerParams(vmem_limit_bytes=32 << 20),
    )(gate, up, down, across(gate_scale), across(up_scale), across(down_scale))


def expert_kernel(groups, upper, recv_ref, gate_ref, up_ref, *rest):
    down_refs, (out_ref, x_ref, h_ref, o_ref) = rest[:PART], rest[PART:]
    width = x_ref.shape[1]
    blocks = recv_ref.shape[0] // 256
    tile = gate_ref.shape[1]
    i = pl.program_id(0)

    @pl.when(i == 0)
    def _():
        row = 0
        start = 0
        for _, size in groups:
            cuts = 8 // size
            piece = width // cuts
            tall = 32 * size
            for b in range(blocks):
                block = recv_ref[b * 256 : (b + 1) * 256, start : start + piece]
                if cuts > 1:
                    block = jnp.dot(turn(size, False), block, preferred_element_type=F32)
                    block = block.astype(BF)
                for c in range(cuts):
                    x_ref[row : row + tall, c * piece : (c + 1) * piece] = block[
                        c * tall : (c + 1) * tall
                    ]
                row += tall
            start += piece

    @pl.when(i < upper)
    def _():
        x = x_ref[...]
        gate = jnp.dot(x, gate_ref[...], preferred_element_type=F32)
        up = jnp.dot(x, up_ref[...], preferred_element_type=F32)
        hidden = gate / (1.0 + jnp.exp(-gate)) * up
        h_ref[:, pl.ds(pl.multiple_of(i * tile, tile), tile)] = hidden.astype(BF)

    @pl.when(i >= upper)
    def _():
        down = jnp.concatenate([ref[...] for ref in down_refs], axis=1)
        o_ref[...] = jnp.dot(h_ref[...], down, preferred_element_type=F32).astype(BF)
        row = 0
        start = 0
        for _, size in groups:
            cuts = 8 // size
            lanes = PART * BLOCK // cuts
            tall = 32 * size
            for b in range(blocks):
                block = jnp.concatenate(
                    [
                        o_ref[row : row + tall, c * lanes : (c + 1) * lanes]
                        for c in range(cuts)
                    ],
                    axis=0,
                )
                if cuts > 1:
                    block = jnp.dot(turn(size, True), block, preferred_element_type=F32)
                    block = block.astype(BF)
                out_ref[b * 256 : (b + 1) * 256, start : start + lanes] = block
                row += tall
            start += lanes


def expert(groups, recv, gate, up, down):
    width, hidden = gate.shape
    tile = 256
    upper = hidden // tile
    steps = width // (PART * BLOCK)
    rows = sum(size for _, size in groups) * recv.shape[0] // 8
    lanes = sum(PART * BLOCK * size // 8 for _, size in groups)
    first_spec = pl.BlockSpec((width, tile), lambda i: (0, jnp.minimum(i, upper - 1)))
    down_spec = lambda q: pl.BlockSpec(
        (hidden, BLOCK), lambda i: (0, q * steps + jnp.maximum(i - upper, 0))
    )
    return pl.pallas_call(
        functools.partial(expert_kernel, groups, upper),
        grid=(upper + steps,),
        out_shape=jax.ShapeDtypeStruct((recv.shape[0], lanes * steps), BF),
        in_specs=[
            pl.BlockSpec(recv.shape, lambda i: (0, 0), pipeline_mode=pl.Buffered(1)),
            first_spec,
            first_spec,
        ]
        + [down_spec(q) for q in range(PART)],
        out_specs=pl.BlockSpec((recv.shape[0], lanes), lambda i: (0, jnp.maximum(i - upper, 0))),
        scratch_shapes=[
            pltpu.VMEM((rows, width), BF),
            pltpu.VMEM((rows, hidden), BF),
            pltpu.VMEM((rows, PART * BLOCK), BF),
        ],
        compiler_params=pltpu.CompilerParams(vmem_limit_bytes=52 << 20),
    )(recv, gate, up, *([down] * PART))


def merge_kernel(groups, more, recv_ref, *rest):
    tables_, rest = rest[: len(groups)], rest[len(groups) :]
    out_ref = rest[-1]
    tokens, width = out_ref.shape
    quarter = width // PART
    t = pl.program_id(0)
    sums = [jnp.zeros((tokens, BLOCK), F32) for _ in range(PART)]
    start = 0
    for (_, size), table_ref in zip(groups, tables_):
        cuts = 8 // size
        lanes = PART * BLOCK // cuts
        got = jnp.dot(
            table_ref[...], recv_ref[:, start : start + lanes], preferred_element_type=F32
        )
        start += lanes
        for c in range(cuts):
            both = got[2 * c * tokens : (2 * c + 1) * tokens] + got[
                (2 * c + 1) * tokens : (2 * c + 2) * tokens
            ]
            for p in range(lanes // BLOCK):
                q = c * (PART // cuts) + p
                sums[q] = sums[q] + both[:, p * BLOCK : (p + 1) * BLOCK]
    for q in range(PART):
        at = pl.ds(pl.multiple_of(q * quarter + t * BLOCK, BLOCK), BLOCK)
        total = sums[q]
        if more:
            total = total + rest[0][:, at]
        out_ref[:, at] = total.astype(out_ref.dtype)


def merge(groups, recv, tables_, dtype, before=None):
    steps = 7
    lanes = recv.shape[1] // steps
    tokens = recv.shape[0] // 8
    width = steps * PART * BLOCK
    whole = lambda shape: pl.BlockSpec(shape, lambda t: (0, 0), pipeline_mode=pl.Buffered(1))
    more = before is not None
    return pl.pallas_call(
        functools.partial(merge_kernel, groups, more),
        grid=(steps,),
        out_shape=jax.ShapeDtypeStruct((tokens, width), dtype),
        in_specs=[pl.BlockSpec((recv.shape[0], lanes), lambda t: (0, t))]
        + [whole(table.shape) for table in tables_]
        + ([whole((tokens, width))] if more else []),
        out_specs=pl.BlockSpec((tokens, width), lambda t: (0, 0)),
        compiler_params=pltpu.CompilerParams(vmem_limit_bytes=32 << 20),
    )(recv, *tables_, *((before,) if more else ()))


def exchange(block):
    rows, wide = block.shape
    block = lax.all_to_all(
        block.reshape(rows // 8, 8, wide), AXES, split_axis=0, concat_axis=0, tiled=True
    )
    return block.reshape(rows, wide)


def local(
    tokens, act_scale, routes, combine, w_gate, gate_scale, w_up, up_scale, w_down, down_scale
):
    route_count = routes.shape[1]
    experts = lax.axis_size("node") * lax.axis_size("local")
    capacity = 5 * tokens.shape[0] * route_count // (4 * experts)
    one, two = groups_of(0, FIRST), groups_of(FIRST, capacity)
    names, scale = routes.T, act_scale.T
    send_one = pack(one, tokens, scale, names)
    recv_one = exchange(send_one)
    send_two = pack(two, tokens, scale, names)
    weights = dequantize(w_gate[0], w_up[0], w_down[0], gate_scale[0], up_scale[0], down_scale[0])
    found = tables((one, two), names, combine.T)
    recv_two = exchange(send_two)
    done_one = expert(one, recv_one, *weights)
    back_one = exchange(done_one)
    done_two = expert(two, recv_two, *weights)
    back_two = exchange(done_two)
    total = merge(one, back_one, found[: len(one)], F32)
    return merge(two, back_two, found[len(one) :], BF, total)


def solution(mesh):
    placed = (P(AXES, None),) * 4 + (P(AXES, None, None),) * 6
    return jax.shard_map(
        local, mesh=mesh, in_specs=placed, out_specs=P(AXES, None), check_vma=False
    )
```

```python
import functools

import jax
import jax.numpy as jnp
from jax import lax
from jax.experimental import pallas as pl
from jax.experimental.pallas import tpu as pltpu
from jax.sharding import PartitionSpec as P


AXES = ("node", "local")
BLOCK = 128
PART = 4
FIRST = 6
BF = jnp.bfloat16
F32 = jnp.float32


def groups_of(first, last):
    groups = []
    for size in (8, 4, 2):
        while last - first >= size:
            groups.append((first, size))
            first += size
    return groups


def ranks(names):
    count, rows = names.shape
    expert = lax.broadcasted_iota(jnp.int32, (rows, rows), 0)
    named = jnp.zeros((rows, rows), F32)
    for k in range(count):
        named = named + jnp.where(names[k : k + 1, :] == expert, 1.0, 0.0)
    later = lax.broadcasted_iota(jnp.int32, (rows, rows), 0) < lax.broadcasted_iota(
        jnp.int32, (rows, rows), 1
    )
    before = jnp.dot(
        named.astype(BF), jnp.where(later, 1.0, 0.0).astype(BF), preferred_element_type=F32
    )
    return jnp.where(named > 0.5, before, -1.0)


def eightfold(table):
    rows, cols = table.shape
    return jnp.broadcast_to(table[:, None, :], (rows, 8, cols)).reshape(rows * 8, cols)


def places(shape, size):
    row = lax.broadcasted_iota(jnp.int32, shape, 0)
    return (row & (size - 1)).astype(F32), (row & 7) >> (size.bit_length() - 1)


def turn(size, back):
    shape = (256, 256)
    out = lax.broadcasted_iota(jnp.int32, shape, 1 if back else 0)
    held = lax.broadcasted_iota(jnp.int32, shape, 0 if back else 1)
    low = size.bit_length() - 1
    piece = out >> (5 + low)
    source = (out >> low) & 31
    slot = out & (size - 1)
    return jnp.where(held == source * 8 + piece * size + slot, 1.0, 0.0).astype(BF)


def pieces_of(groups, width):
    out = []
    for at, (_, size) in enumerate(groups):
        piece = width * size // 8
        for start in range(0, piece, 4 * BLOCK):
            out.append((at, start, min(4 * BLOCK, piece - start)))
    return out


def pack_kernel(groups, tokens_hbm, scale_hbm, names_hbm, out_hbm, *scratch):
    tokens_ref, scale_ref, names_ref, out_ref, in_sems, out_sems = scratch
    arrivals = [
        pltpu.make_async_copy(source, target, in_sems.at[n])
        for n, (source, target) in enumerate(
            (
                (names_hbm, names_ref),
                (scale_hbm, scale_ref),
                (tokens_hbm, tokens_ref),
            )
        )
    ]
    for copy in arrivals:
        copy.start()
    _, width = tokens_ref.shape
    blocks = scale_ref.shape[0]
    arrivals[0].wait()
    held = eightfold(ranks(names_ref[...]))
    found = []
    for first, size in groups:
        slot, cut = places(held.shape, size)
        match = held == slot + float(first)
        found.append(
            jnp.concatenate(
                [jnp.where(match & (cut == c), 1.0, 0.0).astype(BF) for c in range(8 // size)],
                axis=1,
            )
        )
    lane = lax.broadcasted_iota(jnp.int32, (blocks, width), 1)
    spread = jnp.where(
        (lane >> 7) == lax.broadcasted_iota(jnp.int32, (blocks, width), 0), 1.0, 0.0
    ).astype(BF)
    arrivals[1].wait()
    scale = lax.dot_general(
        scale_ref[...].astype(BF), spread, (((0,), (0,)), ((), ())), preferred_element_type=F32
    )
    arrivals[2].wait()
    inputs = (tokens_ref[...].astype(F32) * scale).astype(BF)
    begin = 0
    departures = []
    for n, (at, start, lanes) in enumerate(pieces_of(groups, width)):
        size = groups[at][1]
        piece = width * size // 8
        stacked = jnp.concatenate(
            [
                inputs[:, c * piece + start : c * piece + start + lanes]
                for c in range(8 // size)
            ],
            axis=0,
        )
        part = slice(begin, begin + lanes)
        out_ref[:, part] = jnp.dot(found[at], stacked, preferred_element_type=F32).astype(BF)
        copy = pltpu.make_async_copy(out_ref.at[:, part], out_hbm.at[:, part], out_sems.at[n])
        copy.start()
        departures.append(copy)
        begin += lanes
    for copy in departures:
        copy.wait()


def pack(groups, tokens, scale, names):
    rows, width = tokens.shape
    wide = sum(width * size // 8 for _, size in groups)
    return pl.pallas_call(
        functools.partial(pack_kernel, groups),
        out_shape=pltpu.HBM((rows * 8, wide), BF),
        in_specs=[pl.BlockSpec(memory_space=pltpu.HBM)] * 3,
        out_specs=pl.BlockSpec(memory_space=pltpu.HBM),
        scratch_shapes=[
            pltpu.VMEM(tokens.shape, tokens.dtype),
            pltpu.VMEM(scale.shape, scale.dtype),
            pltpu.VMEM(names.shape, names.dtype),
            pltpu.VMEM((rows * 8, wide), BF),
            pltpu.SemaphoreType.DMA((3,)),
            pltpu.SemaphoreType.DMA((len(pieces_of(groups, width)),)),
        ],
        compiler_params=pltpu.CompilerParams(vmem_limit_bytes=40 << 20),
    )(*(pltpu.with_memory_space_constraint(x, pltpu.HBM) for x in (tokens, scale, names)))


def table_kernel(chunks, names_ref, weight_ref, *out_refs):
    names = names_ref[...]
    held = ranks(names)
    rows = held.shape[0]
    expert = lax.broadcasted_iota(jnp.int32, (rows, rows), 0)
    weight = jnp.zeros((rows, rows), F32)
    for k in range(names.shape[0]):
        weight = weight + jnp.where(names[k : k + 1, :] == expert, weight_ref[k : k + 1, :], 0.0)
    held, weight = eightfold(held), eightfold(weight)
    at = 0
    for groups in chunks:
        for first, size in groups:
            slot, cut = places(held.shape, size)
            match = held == slot + float(first)
            for c in range(8 // size):
                own = jnp.where(match & (cut == c), weight, 0.0).T
                high = own.astype(BF)
                low = (own - high.astype(F32)).astype(BF)
                out_refs[at][2 * c * rows : (2 * c + 1) * rows, :] = high
                out_refs[at][(2 * c + 1) * rows : (2 * c + 2) * rows, :] = low
            at += 1


def tables(chunks, names, weight):
    rows = names.shape[1]
    return pl.pallas_call(
        functools.partial(table_kernel, chunks),
        out_shape=[
            jax.ShapeDtypeStruct((2 * (8 // size) * rows, 8 * rows), BF)
            for groups in chunks
            for _, size in groups
        ],
        in_specs=[pl.BlockSpec(memory_space=pltpu.VMEM)] * 2,
        out_specs=[pl.BlockSpec(memory_space=pltpu.VMEM)] * sum(len(g) for g in chunks),
        compiler_params=pltpu.CompilerParams(vmem_limit_bytes=40 << 20),
    )(names, weight)


def dequantize_kernel(gate_ref, up_ref, down_ref, gs_ref, us_ref, ds_ref, g_ref, u_ref, d_ref):
    for weight_ref, scale_ref, out_ref in (
        (gate_ref, gs_ref, g_ref),
        (up_ref, us_ref, u_ref),
        (down_ref, ds_ref, d_ref),
    ):
        for k in range(weight_ref.shape[0] // BLOCK):
            part = slice(k * BLOCK, (k + 1) * BLOCK)
            out_ref[part, :] = (weight_ref[part, :].astype(F32) * scale_ref[k]).astype(BF)


def dequantize(gate, up, down, gate_scale, up_scale, down_scale):
    width, hidden = gate.shape
    steps = 7
    tall, wide = width // steps, width // steps
    across = lambda scale: jnp.repeat(scale, BLOCK, axis=1)[:, None, :]
    row_spec = pl.BlockSpec((tall, hidden), lambda i: (i, 0))
    col_spec = pl.BlockSpec((hidden, wide), lambda i: (0, i))
    row_scale = pl.BlockSpec((tall // BLOCK, 1, hidden), lambda i: (i, 0, 0))
    col_scale = pl.BlockSpec((hidden // BLOCK, 1, wide), lambda i: (0, 0, i))
    return pl.pallas_call(
        dequantize_kernel,
        grid=(steps,),
        out_shape=[jax.ShapeDtypeStruct(w.shape, BF) for w in (gate, up, down)],
        in_specs=[row_spec, row_spec, col_spec, row_scale, row_scale, col_scale],
        out_specs=[row_spec, row_spec, col_spec],
        compiler_params=pltpu.CompilerParams(vmem_limit_bytes=32 << 20),
    )(gate, up, down, across(gate_scale), across(up_scale), across(down_scale))


def expert_kernel(groups, upper, recv_ref, gate_ref, up_ref, *rest):
    down_refs, (out_ref, x_ref, h_ref, o_ref) = rest[:PART], rest[PART:]
    width = x_ref.shape[1]
    blocks = recv_ref.shape[0] // 256
    tile = gate_ref.shape[1]
    i = pl.program_id(0)

    @pl.when(i == 0)
    def _():
        row = 0
        start = 0
        for _, size in groups:
            cuts = 8 // size
            piece = width // cuts
            tall = 32 * size
            for b in range(blocks):
                block = recv_ref[b * 256 : (b + 1) * 256, start : start + piece]
                if cuts > 1:
                    block = jnp.dot(turn(size, False), block, preferred_element_type=F32)
                    block = block.astype(BF)
                for c in range(cuts):
                    x_ref[row : row + tall, c * piece : (c + 1) * piece] = block[
                        c * tall : (c + 1) * tall
                    ]
                row += tall
            start += piece

    @pl.when(i < upper)
    def _():
        x = x_ref[...]
        gate = jnp.dot(x, gate_ref[...], preferred_element_type=F32)
        up = jnp.dot(x, up_ref[...], preferred_element_type=F32)
        hidden = gate / (1.0 + jnp.exp(-gate)) * up
        h_ref[:, pl.ds(pl.multiple_of(i * tile, tile), tile)] = hidden.astype(BF)

    @pl.when(i >= upper)
    def _():
        down = jnp.concatenate([ref[...] for ref in down_refs], axis=1)
        o_ref[...] = jnp.dot(h_ref[...], down, preferred_element_type=F32).astype(BF)
        row = 0
        start = 0
        for _, size in groups:
            cuts = 8 // size
            lanes = PART * BLOCK // cuts
            tall = 32 * size
            for b in range(blocks):
                block = jnp.concatenate(
                    [
                        o_ref[row : row + tall, c * lanes : (c + 1) * lanes]
                        for c in range(cuts)
                    ],
                    axis=0,
                )
                if cuts > 1:
                    block = jnp.dot(turn(size, True), block, preferred_element_type=F32)
                    block = block.astype(BF)
                out_ref[b * 256 : (b + 1) * 256, start : start + lanes] = block
                row += tall
            start += lanes


def expert(groups, recv, gate, up, down):
    width, hidden = gate.shape
    tile = 256
    upper = hidden // tile
    steps = width // (PART * BLOCK)
    rows = sum(size for _, size in groups) * recv.shape[0] // 8
    lanes = sum(PART * BLOCK * size // 8 for _, size in groups)
    first_spec = pl.BlockSpec((width, tile), lambda i: (0, jnp.minimum(i, upper - 1)))
    down_spec = lambda q: pl.BlockSpec(
        (hidden, BLOCK), lambda i: (0, q * steps + jnp.maximum(i - upper, 0))
    )
    return pl.pallas_call(
        functools.partial(expert_kernel, groups, upper),
        grid=(upper + steps,),
        out_shape=jax.ShapeDtypeStruct((recv.shape[0], lanes * steps), BF),
        in_specs=[
            pl.BlockSpec(recv.shape, lambda i: (0, 0), pipeline_mode=pl.Buffered(1)),
            first_spec,
            first_spec,
        ]
        + [down_spec(q) for q in range(PART)],
        out_specs=pl.BlockSpec((recv.shape[0], lanes), lambda i: (0, jnp.maximum(i - upper, 0))),
        scratch_shapes=[
            pltpu.VMEM((rows, width), BF),
            pltpu.VMEM((rows, hidden), BF),
            pltpu.VMEM((rows, PART * BLOCK), BF),
        ],
        compiler_params=pltpu.CompilerParams(vmem_limit_bytes=52 << 20),
    )(recv, gate, up, *([down] * PART))


def merge_kernel(groups, recv_ref, *rest):
    tables_, out_ref = rest[:-1], rest[-1]
    tokens, width = out_ref.shape
    quarter = width // PART
    t = pl.program_id(0)
    sums = [jnp.zeros((tokens, BLOCK), F32) for _ in range(PART)]
    start = 0
    for (_, size), table_ref in zip(groups, tables_):
        cuts = 8 // size
        lanes = PART * BLOCK // cuts
        got = jnp.dot(
            table_ref[...], recv_ref[:, start : start + lanes], preferred_element_type=F32
        )
        start += lanes
        for c in range(cuts):
            both = got[2 * c * tokens : (2 * c + 1) * tokens] + got[
                (2 * c + 1) * tokens : (2 * c + 2) * tokens
            ]
            for p in range(lanes // BLOCK):
                q = c * (PART // cuts) + p
                sums[q] = sums[q] + both[:, p * BLOCK : (p + 1) * BLOCK]
    for q in range(PART):
        at = pl.ds(pl.multiple_of(q * quarter + t * BLOCK, BLOCK), BLOCK)
        out_ref[:, at] = sums[q]


def merge(groups, recv, tables_):
    steps = 7
    lanes = recv.shape[1] // steps
    tokens = recv.shape[0] // 8
    width = steps * PART * BLOCK
    whole = lambda shape: pl.BlockSpec(shape, lambda t: (0, 0), pipeline_mode=pl.Buffered(1))
    return pl.pallas_call(
        functools.partial(merge_kernel, groups),
        grid=(steps,),
        out_shape=jax.ShapeDtypeStruct((tokens, width), F32),
        in_specs=[pl.BlockSpec((recv.shape[0], lanes), lambda t: (0, t))]
        + [whole(table.shape) for table in tables_],
        out_specs=pl.BlockSpec((tokens, width), lambda t: (0, 0)),
        compiler_params=pltpu.CompilerParams(vmem_limit_bytes=32 << 20),
    )(recv, *tables_)


def finish_kernel(groups, table_refs, before_ref, recv_hbm, out_hbm, recv_ref, out_ref, *sems):
    in_sems, out_sems = sems
    steps, _, lanes = recv_ref.shape
    tokens, width = out_ref.shape
    quarter = width // PART
    arrivals = [
        pltpu.make_async_copy(
            recv_hbm.at[:, t * lanes : (t + 1) * lanes], recv_ref.at[t], in_sems.at[t]
        )
        for t in range(steps)
    ]
    for copy in arrivals:
        copy.start()
    departures = []
    for t in range(steps):
        arrivals[t].wait()
        sums = [None] * PART
        start = 0
        for (_, size), table_ref in zip(groups, table_refs):
            cuts = 8 // size
            wide = PART * BLOCK // cuts
            got = jnp.dot(
                table_ref[...], recv_ref[t, :, start : start + wide], preferred_element_type=F32
            )
            start += wide
            for c in range(cuts):
                both = got[2 * c * tokens : (2 * c + 1) * tokens] + got[
                    (2 * c + 1) * tokens : (2 * c + 2) * tokens
                ]
                for p in range(wide // BLOCK):
                    q = c * (PART // cuts) + p
                    own = both[:, p * BLOCK : (p + 1) * BLOCK]
                    sums[q] = own if sums[q] is None else sums[q] + own
        for q in range(PART):
            part = slice(q * quarter + t * BLOCK, q * quarter + (t + 1) * BLOCK)
            out_ref[:, part] = (sums[q] + before_ref[:, part]).astype(out_ref.dtype)
            copy = pltpu.make_async_copy(
                out_ref.at[:, part], out_hbm.at[:, part], out_sems.at[t * PART + q]
            )
            copy.start()
            departures.append(copy)
    for copy in departures:
        copy.wait()


def finish(groups, recv, tables_, before):
    tokens, width = before.shape
    steps = width // (PART * BLOCK)
    lanes = recv.shape[1] // steps
    count = len(tables_)

    def kernel(*refs):
        finish_kernel(groups, refs[:count], *refs[count:])

    return pl.pallas_call(
        kernel,
        out_shape=pltpu.HBM((tokens, width), BF),
        in_specs=[pl.BlockSpec(memory_space=pltpu.VMEM)] * (count + 1)
        + [pl.BlockSpec(memory_space=pltpu.HBM)],
        out_specs=pl.BlockSpec(memory_space=pltpu.HBM),
        scratch_shapes=[
            pltpu.VMEM((steps, recv.shape[0], lanes), BF),
            pltpu.VMEM((tokens, width), BF),
            pltpu.SemaphoreType.DMA((steps,)),
            pltpu.SemaphoreType.DMA((steps * PART,)),
        ],
        compiler_params=pltpu.CompilerParams(vmem_limit_bytes=32 << 20),
    )(*tables_, before, recv)


def exchange(block):
    rows, wide = block.shape
    block = lax.all_to_all(
        block.reshape(rows // 8, 8, wide), AXES, split_axis=0, concat_axis=0, tiled=True
    )
    return block.reshape(rows, wide)


def local(
    tokens, act_scale, routes, combine, w_gate, gate_scale, w_up, up_scale, w_down, down_scale
):
    route_count = routes.shape[1]
    experts = lax.axis_size("node") * lax.axis_size("local")
    capacity = 5 * tokens.shape[0] * route_count // (4 * experts)
    one, two = groups_of(0, FIRST), groups_of(FIRST, capacity)
    names, scale = routes.T, act_scale.T
    send_one = pack(one, tokens, scale, names)
    recv_one = exchange(send_one)
    send_two = pack(two, tokens, scale, names)
    weights = dequantize(w_gate[0], w_up[0], w_down[0], gate_scale[0], up_scale[0], down_scale[0])
    found = tables((one, two), names, combine.T)
    recv_two = exchange(send_two)
    done_one = expert(one, recv_one, *weights)
    back_one = exchange(done_one)
    done_two = expert(two, recv_two, *weights)
    back_two = exchange(done_two)
    total = merge(one, back_one, found[: len(one)])
    return finish(two, back_two, found[len(one) :], total)


def solution(mesh):
    placed = (P(AXES, None),) * 4 + (P(AXES, None, None),) * 6
    return jax.shard_map(
        local, mesh=mesh, in_specs=placed, out_specs=P(AXES, None), check_vma=False
    )
```

```python
import functools

import jax
import jax.numpy as jnp
from jax import lax
from jax.experimental import pallas as pl
from jax.experimental.pallas import tpu as pltpu
from jax.sharding import PartitionSpec as P


AXES = ("node", "local")
BLOCK = 128
PART = 4
FIRST = 6
BF = jnp.bfloat16
F32 = jnp.float32


def groups_of(first, last):
    groups = []
    for size in (8, 4, 2):
        while last - first >= size:
            groups.append((first, size))
            first += size
    return groups


def ranks(names):
    count, rows = names.shape
    expert = lax.broadcasted_iota(jnp.int32, (rows, rows), 0)
    named = jnp.zeros((rows, rows), F32)
    for k in range(count):
        named = named + jnp.where(names[k : k + 1, :] == expert, 1.0, 0.0)
    later = lax.broadcasted_iota(jnp.int32, (rows, rows), 0) < lax.broadcasted_iota(
        jnp.int32, (rows, rows), 1
    )
    before = jnp.dot(
        named.astype(BF), jnp.where(later, 1.0, 0.0).astype(BF), preferred_element_type=F32
    )
    return jnp.where(named > 0.5, before, -1.0)


def eightfold(table):
    rows, cols = table.shape
    return jnp.broadcast_to(table[:, None, :], (rows, 8, cols))


def wanted(cols, first, size, cut):
    row = lax.broadcasted_iota(jnp.int32, (1, 8, cols), 1)
    slot = (row & (size - 1)) + first
    return jnp.where(row >> (size.bit_length() - 1) == cut, slot, -2).astype(F32)


def turn(size, back):
    shape = (256, 256)
    out = lax.broadcasted_iota(jnp.int32, shape, 1 if back else 0)
    held = lax.broadcasted_iota(jnp.int32, shape, 0 if back else 1)
    low = size.bit_length() - 1
    piece = out >> (5 + low)
    source = (out >> low) & 31
    slot = out & (size - 1)
    return jnp.where(held == source * 8 + piece * size + slot, 1.0, 0.0).astype(BF)


def pieces_of(groups, width):
    out = []
    for at, (_, size) in enumerate(groups):
        piece = width * size // 8
        for start in range(0, piece, 4 * BLOCK):
            out.append((at, start, min(4 * BLOCK, piece - start)))
    return out


def pack_kernel(groups, tokens_hbm, scale_hbm, names_hbm, out_hbm, *scratch):
    tokens_ref, scale_ref, names_ref, out_ref, in_sems, out_sems = scratch
    arrivals = [
        pltpu.make_async_copy(source, target, in_sems.at[n])
        for n, (source, target) in enumerate(
            (
                (names_hbm, names_ref),
                (scale_hbm, scale_ref),
                (tokens_hbm, tokens_ref),
            )
        )
    ]
    for copy in arrivals:
        copy.start()
    _, width = tokens_ref.shape
    blocks = scale_ref.shape[0]
    arrivals[0].wait()
    held = eightfold(ranks(names_ref[...]))
    found = []
    for first, size in groups:
        found.append(
            jnp.concatenate(
                [
                    jnp.where(held == wanted(held.shape[2], first, size, c), 1.0, 0.0)
                    .astype(BF)
                    .reshape(-1, held.shape[2])
                    for c in range(8 // size)
                ],
                axis=1,
            )
        )
    lane = lax.broadcasted_iota(jnp.int32, (blocks, width), 1)
    spread = jnp.where(
        (lane >> 7) == lax.broadcasted_iota(jnp.int32, (blocks, width), 0), 1.0, 0.0
    ).astype(BF)
    arrivals[1].wait()
    scale = lax.dot_general(
        scale_ref[...].astype(BF), spread, (((0,), (0,)), ((), ())), preferred_element_type=F32
    )
    arrivals[2].wait()
    inputs = tokens_ref[...] * scale.astype(BF)
    begin = 0
    departures = []
    for n, (at, start, lanes) in enumerate(pieces_of(groups, width)):
        size = groups[at][1]
        piece = width * size // 8
        stacked = jnp.concatenate(
            [
                inputs[:, c * piece + start : c * piece + start + lanes]
                for c in range(8 // size)
            ],
            axis=0,
        )
        part = slice(begin, begin + lanes)
        out_ref[:, part] = jnp.dot(found[at], stacked, preferred_element_type=F32).astype(BF)
        copy = pltpu.make_async_copy(out_ref.at[:, part], out_hbm.at[:, part], out_sems.at[n])
        copy.start()
        departures.append(copy)
        begin += lanes
    for copy in departures:
        copy.wait()


def pack(groups, tokens, scale, names):
    rows, width = tokens.shape
    wide = sum(width * size // 8 for _, size in groups)
    return pl.pallas_call(
        functools.partial(pack_kernel, groups),
        out_shape=pltpu.HBM((rows * 8, wide), BF),
        in_specs=[pl.BlockSpec(memory_space=pltpu.HBM)] * 3,
        out_specs=pl.BlockSpec(memory_space=pltpu.HBM),
        scratch_shapes=[
            pltpu.VMEM(tokens.shape, tokens.dtype),
            pltpu.VMEM(scale.shape, scale.dtype),
            pltpu.VMEM(names.shape, names.dtype),
            pltpu.VMEM((rows * 8, wide), BF),
            pltpu.SemaphoreType.DMA((3,)),
            pltpu.SemaphoreType.DMA((len(pieces_of(groups, width)),)),
        ],
        compiler_params=pltpu.CompilerParams(vmem_limit_bytes=40 << 20),
    )(*(pltpu.with_memory_space_constraint(x, pltpu.HBM) for x in (tokens, scale, names)))


def table_kernel(chunks, names_ref, weight_ref, *out_refs):
    names = names_ref[...]
    held = ranks(names)
    rows = held.shape[0]
    expert = lax.broadcasted_iota(jnp.int32, (rows, rows), 0)
    weight = jnp.zeros((rows, rows), F32)
    for k in range(names.shape[0]):
        weight = weight + jnp.where(names[k : k + 1, :] == expert, weight_ref[k : k + 1, :], 0.0)
    held, weight = eightfold(held), eightfold(weight)
    at = 0
    for groups in chunks:
        for first, size in groups:
            for c in range(8 // size):
                match = held == wanted(rows, first, size, c)
                own = jnp.where(match, weight, 0.0).reshape(-1, rows).T
                high = own.astype(BF)
                low = (own - high.astype(F32)).astype(BF)
                out_refs[at][2 * c * rows : (2 * c + 1) * rows, :] = high
                out_refs[at][(2 * c + 1) * rows : (2 * c + 2) * rows, :] = low
            at += 1


def tables(chunks, names, weight):
    rows = names.shape[1]
    return pl.pallas_call(
        functools.partial(table_kernel, chunks),
        out_shape=[
            jax.ShapeDtypeStruct((2 * (8 // size) * rows, 8 * rows), BF)
            for groups in chunks
            for _, size in groups
        ],
        in_specs=[pl.BlockSpec(memory_space=pltpu.VMEM)] * 2,
        out_specs=[pl.BlockSpec(memory_space=pltpu.VMEM)] * sum(len(g) for g in chunks),
        compiler_params=pltpu.CompilerParams(vmem_limit_bytes=40 << 20),
    )(names, weight)


def dequantize_kernel(gate_ref, up_ref, down_ref, gs_ref, us_ref, ds_ref, g_ref, u_ref, d_ref):
    for weight_ref, scale_ref, out_ref in (
        (gate_ref, gs_ref, g_ref),
        (up_ref, us_ref, u_ref),
        (down_ref, ds_ref, d_ref),
    ):
        for k in range(weight_ref.shape[0] // BLOCK):
            part = slice(k * BLOCK, (k + 1) * BLOCK)
            out_ref[part, :] = (weight_ref[part, :].astype(F32) * scale_ref[k]).astype(BF)


def dequantize(gate, up, down, gate_scale, up_scale, down_scale):
    width, hidden = gate.shape
    steps = 7
    tall, wide = width // steps, width // steps
    across = lambda scale: jnp.repeat(scale, BLOCK, axis=1)[:, None, :]
    row_spec = pl.BlockSpec((tall, hidden), lambda i: (i, 0))
    col_spec = pl.BlockSpec((hidden, wide), lambda i: (0, i))
    row_scale = pl.BlockSpec((tall // BLOCK, 1, hidden), lambda i: (i, 0, 0))
    col_scale = pl.BlockSpec((hidden // BLOCK, 1, wide), lambda i: (0, 0, i))
    return pl.pallas_call(
        dequantize_kernel,
        grid=(steps,),
        out_shape=[jax.ShapeDtypeStruct(w.shape, BF) for w in (gate, up, down)],
        in_specs=[row_spec, row_spec, col_spec, row_scale, row_scale, col_scale],
        out_specs=[row_spec, row_spec, col_spec],
        compiler_params=pltpu.CompilerParams(vmem_limit_bytes=32 << 20),
    )(gate, up, down, across(gate_scale), across(up_scale), across(down_scale))


def expert_kernel(groups, upper, recv_ref, gate_ref, up_ref, *rest):
    down_refs, (out_ref, x_ref, h_ref, o_ref) = rest[:PART], rest[PART:]
    width = x_ref.shape[1]
    blocks = recv_ref.shape[0] // 256
    tile = gate_ref.shape[1]
    i = pl.program_id(0)

    @pl.when(i == 0)
    def _():
        row = 0
        start = 0
        for _, size in groups:
            cuts = 8 // size
            piece = width // cuts
            tall = 32 * size
            for b in range(blocks):
                block = recv_ref[b * 256 : (b + 1) * 256, start : start + piece]
                if cuts > 1:
                    block = jnp.dot(turn(size, False), block, preferred_element_type=F32)
                    block = block.astype(BF)
                for c in range(cuts):
                    x_ref[row : row + tall, c * piece : (c + 1) * piece] = block[
                        c * tall : (c + 1) * tall
                    ]
                row += tall
            start += piece

    @pl.when(i < upper)
    def _():
        x = x_ref[...]
        gate = jnp.dot(x, gate_ref[...], preferred_element_type=F32)
        up = jnp.dot(x, up_ref[...], preferred_element_type=F32)
        hidden = gate / (1.0 + jnp.exp(-gate)) * up
        h_ref[:, pl.ds(pl.multiple_of(i * tile, tile), tile)] = hidden.astype(BF)

    @pl.when(i >= upper)
    def _():
        down = jnp.concatenate([ref[...] for ref in down_refs], axis=1)
        o_ref[...] = jnp.dot(h_ref[...], down, preferred_element_type=F32).astype(BF)
        row = 0
        start = 0
        for _, size in groups:
            cuts = 8 // size
            lanes = PART * BLOCK // cuts
            tall = 32 * size
            for b in range(blocks):
                block = jnp.concatenate(
                    [
                        o_ref[row : row + tall, c * lanes : (c + 1) * lanes]
                        for c in range(cuts)
                    ],
                    axis=0,
                )
                if cuts > 1:
                    block = jnp.dot(turn(size, True), block, preferred_element_type=F32)
                    block = block.astype(BF)
                out_ref[b * 256 : (b + 1) * 256, start : start + lanes] = block
                row += tall
            start += lanes


def expert(groups, recv, gate, up, down):
    width, hidden = gate.shape
    tile = 256
    upper = hidden // tile
    steps = width // (PART * BLOCK)
    rows = sum(size for _, size in groups) * recv.shape[0] // 8
    lanes = sum(PART * BLOCK * size // 8 for _, size in groups)
    first_spec = pl.BlockSpec((width, tile), lambda i: (0, jnp.minimum(i, upper - 1)))
    down_spec = lambda q: pl.BlockSpec(
        (hidden, BLOCK), lambda i: (0, q * steps + jnp.maximum(i - upper, 0))
    )
    return pl.pallas_call(
        functools.partial(expert_kernel, groups, upper),
        grid=(upper + steps,),
        out_shape=jax.ShapeDtypeStruct((recv.shape[0], lanes * steps), BF),
        in_specs=[
            pl.BlockSpec(recv.shape, lambda i: (0, 0), pipeline_mode=pl.Buffered(1)),
            first_spec,
            first_spec,
        ]
        + [down_spec(q) for q in range(PART)],
        out_specs=pl.BlockSpec((recv.shape[0], lanes), lambda i: (0, jnp.maximum(i - upper, 0))),
        scratch_shapes=[
            pltpu.VMEM((rows, width), BF),
            pltpu.VMEM((rows, hidden), BF),
            pltpu.VMEM((rows, PART * BLOCK), BF),
        ],
        compiler_params=pltpu.CompilerParams(vmem_limit_bytes=52 << 20),
    )(recv, gate, up, *([down] * PART))


def merge_kernel(groups, recv_ref, *rest):
    tables_, out_ref = rest[:-1], rest[-1]
    tokens, width = out_ref.shape
    quarter = width // PART
    t = pl.program_id(0)
    sums = [jnp.zeros((tokens, BLOCK), F32) for _ in range(PART)]
    start = 0
    for (_, size), table_ref in zip(groups, tables_):
        cuts = 8 // size
        lanes = PART * BLOCK // cuts
        got = jnp.dot(
            table_ref[...], recv_ref[:, start : start + lanes], preferred_element_type=F32
        )
        start += lanes
        for c in range(cuts):
            both = got[2 * c * tokens : (2 * c + 1) * tokens] + got[
                (2 * c + 1) * tokens : (2 * c + 2) * tokens
            ]
            for p in range(lanes // BLOCK):
                q = c * (PART // cuts) + p
                sums[q] = sums[q] + both[:, p * BLOCK : (p + 1) * BLOCK]
    for q in range(PART):
        at = pl.ds(pl.multiple_of(q * quarter + t * BLOCK, BLOCK), BLOCK)
        out_ref[:, at] = sums[q]


def merge(groups, recv, tables_):
    steps = 7
    lanes = recv.shape[1] // steps
    tokens = recv.shape[0] // 8
    width = steps * PART * BLOCK
    whole = lambda shape: pl.BlockSpec(shape, lambda t: (0, 0), pipeline_mode=pl.Buffered(1))
    return pl.pallas_call(
        functools.partial(merge_kernel, groups),
        grid=(steps,),
        out_shape=jax.ShapeDtypeStruct((tokens, width), F32),
        in_specs=[pl.BlockSpec((recv.shape[0], lanes), lambda t: (0, t))]
        + [whole(table.shape) for table in tables_],
        out_specs=pl.BlockSpec((tokens, width), lambda t: (0, 0)),
        compiler_params=pltpu.CompilerParams(vmem_limit_bytes=32 << 20),
    )(recv, *tables_)


def finish_kernel(groups, spans, table_refs, before_ref, recv_hbm, out_hbm, *scratch):
    recv_ref, out_ref, in_sems, out_sems = scratch
    tokens, width = out_ref.shape
    quarter = width // PART
    lanes = recv_ref.shape[1] * PART * BLOCK // width
    arrivals = []
    for n, (low, high) in enumerate(spans):
        part = slice(low * lanes, high * lanes)
        arrivals.append(
            pltpu.make_async_copy(recv_hbm.at[:, part], recv_ref.at[:, part], in_sems.at[n])
        )
        arrivals[-1].start()
    departures = []
    for n, (low, high) in enumerate(spans):
        arrivals[n].wait()
        start = 0
        for (_, size), table_ref in zip(groups, table_refs):
            cuts = 8 // size
            wide = PART * BLOCK // cuts
            for c in range(cuts):
                table = table_ref[2 * c * tokens : 2 * (c + 1) * tokens, :]
                got = jnp.concatenate(
                    [
                        recv_ref[:, t * lanes + start : t * lanes + start + wide]
                        for t in range(low, high)
                    ],
                    axis=1,
                )
                got = jnp.dot(table, got, preferred_element_type=F32)
                both = got[:tokens] + got[tokens:]
                for t in range(low, high):
                    for p in range(wide // BLOCK):
                        q = c * (PART // cuts) + p
                        part = slice(q * quarter + t * BLOCK, q * quarter + (t + 1) * BLOCK)
                        lane = (t - low) * wide + p * BLOCK
                        own = both[:, lane : lane + BLOCK] + before_ref[:, part]
                        out_ref[:, part] = own.astype(out_ref.dtype)
            start += wide
        for q in range(PART):
            part = slice(q * quarter + low * BLOCK, q * quarter + high * BLOCK)
            copy = pltpu.make_async_copy(
                out_ref.at[:, part], out_hbm.at[:, part], out_sems.at[n * PART + q]
            )
            copy.start()
            departures.append(copy)
    for copy in departures:
        copy.wait()


def finish(groups, recv, tables_, before):
    tokens, width = before.shape
    assert len(groups) == 1
    spans = ((0, 2), (2, 5), (5, 7))

    def kernel(*refs):
        finish_kernel(groups, spans, refs[:1], *refs[1:])

    return pl.pallas_call(
        kernel,
        out_shape=pltpu.HBM((tokens, width), BF),
        in_specs=[pl.BlockSpec(memory_space=pltpu.VMEM)] * 2
        + [pl.BlockSpec(memory_space=pltpu.HBM)],
        out_specs=pl.BlockSpec(memory_space=pltpu.HBM),
        scratch_shapes=[
            pltpu.VMEM(recv.shape, BF),
            pltpu.VMEM((tokens, width), BF),
            pltpu.SemaphoreType.DMA((len(spans),)),
            pltpu.SemaphoreType.DMA((len(spans) * PART,)),
        ],
        compiler_params=pltpu.CompilerParams(vmem_limit_bytes=32 << 20),
    )(*tables_, before, recv)


def exchange(block):
    rows, wide = block.shape
    block = lax.all_to_all(
        block.reshape(rows // 8, 8, wide), AXES, split_axis=0, concat_axis=0, tiled=True
    )
    return block.reshape(rows, wide)


def local(
    tokens, act_scale, routes, combine, w_gate, gate_scale, w_up, up_scale, w_down, down_scale
):
    route_count = routes.shape[1]
    experts = lax.axis_size("node") * lax.axis_size("local")
    capacity = 5 * tokens.shape[0] * route_count // (4 * experts)
    one, two = groups_of(0, FIRST), groups_of(FIRST, capacity)
    names, scale = routes.T, act_scale.T
    send_one = pack(one, tokens, scale, names)
    recv_one = exchange(send_one)
    send_two = pack(two, tokens, scale, names)
    weights = dequantize(w_gate[0], w_up[0], w_down[0], gate_scale[0], up_scale[0], down_scale[0])
    found = tables((one, two), names, combine.T)
    recv_two = exchange(send_two)
    done_one = expert(one, recv_one, *weights)
    back_one = exchange(done_one)
    done_two = expert(two, recv_two, *weights)
    back_two = exchange(done_two)
    total = merge(one, back_one, found[: len(one)])
    return finish(two, back_two, found[len(one) :], total)


def solution(mesh):
    placed = (P(AXES, None),) * 4 + (P(AXES, None, None),) * 6
    return jax.shard_map(
        local, mesh=mesh, in_specs=placed, out_specs=P(AXES, None), check_vma=False
    )
```

```python
import functools

import jax
import jax.numpy as jnp
from jax import lax
from jax.experimental import pallas as pl
from jax.experimental.pallas import tpu as pltpu
from jax.sharding import PartitionSpec as P


AXES = ("node", "local")
BLOCK = 128
PART = 4
FIRST = 6
BF = jnp.bfloat16
F32 = jnp.float32


def groups_of(first, last):
    groups = []
    for size in (8, 4, 2):
        while last - first >= size:
            groups.append((first, size))
            first += size
    return groups


def ranks(names):
    count, rows = names.shape
    expert = lax.broadcasted_iota(jnp.int32, (rows, rows), 0)
    named = jnp.zeros((rows, rows), F32)
    for k in range(count):
        named = named + jnp.where(names[k : k + 1, :] == expert, 1.0, 0.0)
    later = lax.broadcasted_iota(jnp.int32, (rows, rows), 0) < lax.broadcasted_iota(
        jnp.int32, (rows, rows), 1
    )
    before = jnp.dot(
        named.astype(BF), jnp.where(later, 1.0, 0.0).astype(BF), preferred_element_type=F32
    )
    return jnp.where(named > 0.5, before, -1.0)


def eightfold(table):
    rows, cols = table.shape
    return jnp.broadcast_to(table[:, None, :], (rows, 8, cols))


def wanted(cols, first, size, cut):
    row = lax.broadcasted_iota(jnp.int32, (1, 8, cols), 1)
    slot = (row & (size - 1)) + first
    return jnp.where(row >> (size.bit_length() - 1) == cut, slot, -2).astype(F32)


def turn(size, back):
    shape = (256, 256)
    out = lax.broadcasted_iota(jnp.int32, shape, 1 if back else 0)
    held = lax.broadcasted_iota(jnp.int32, shape, 0 if back else 1)
    low = size.bit_length() - 1
    piece = out >> (5 + low)
    source = (out >> low) & 31
    slot = out & (size - 1)
    return jnp.where(held == source * 8 + piece * size + slot, 1.0, 0.0).astype(BF)


def pieces_of(groups, width):
    out = []
    for at, (_, size) in enumerate(groups):
        piece = width * size // 8
        for start in range(0, piece, 4 * BLOCK):
            out.append((at, start, min(4 * BLOCK, piece - start)))
    return out


def pack_kernel(groups, tokens_hbm, scale_hbm, names_hbm, out_hbm, *scratch):
    tokens_ref, scale_ref, names_ref, out_ref, in_sems, out_sems = scratch
    arrivals = [
        pltpu.make_async_copy(source, target, in_sems.at[n])
        for n, (source, target) in enumerate(
            (
                (names_hbm, names_ref),
                (scale_hbm, scale_ref),
                (tokens_hbm, tokens_ref),
            )
        )
    ]
    for copy in arrivals:
        copy.start()
    _, width = tokens_ref.shape
    blocks = scale_ref.shape[0]
    arrivals[0].wait()
    held = eightfold(ranks(names_ref[...]))
    found = []
    for first, size in groups:
        found.append(
            jnp.concatenate(
                [
                    jnp.where(held == wanted(held.shape[2], first, size, c), 1.0, 0.0)
                    .astype(BF)
                    .reshape(-1, held.shape[2])
                    for c in range(8 // size)
                ],
                axis=1,
            )
        )
    lane = lax.broadcasted_iota(jnp.int32, (blocks, width), 1)
    spread = jnp.where(
        (lane >> 7) == lax.broadcasted_iota(jnp.int32, (blocks, width), 0), 1.0, 0.0
    ).astype(BF)
    arrivals[1].wait()
    scale = lax.dot_general(
        scale_ref[...].astype(BF), spread, (((0,), (0,)), ((), ())), preferred_element_type=F32
    )
    arrivals[2].wait()
    inputs = tokens_ref[...] * scale.astype(BF)
    begin = 0
    departures = []
    for n, (at, start, lanes) in enumerate(pieces_of(groups, width)):
        size = groups[at][1]
        piece = width * size // 8
        stacked = jnp.concatenate(
            [
                inputs[:, c * piece + start : c * piece + start + lanes]
                for c in range(8 // size)
            ],
            axis=0,
        )
        part = slice(begin, begin + lanes)
        out_ref[:, part] = jnp.dot(found[at], stacked, preferred_element_type=F32).astype(BF)
        copy = pltpu.make_async_copy(out_ref.at[:, part], out_hbm.at[:, part], out_sems.at[n])
        copy.start()
        departures.append(copy)
        begin += lanes
    for copy in departures:
        copy.wait()


def pack(groups, tokens, scale, names):
    rows, width = tokens.shape
    wide = sum(width * size // 8 for _, size in groups)
    return pl.pallas_call(
        functools.partial(pack_kernel, groups),
        out_shape=pltpu.HBM((rows * 8, wide), BF),
        in_specs=[pl.BlockSpec(memory_space=pltpu.HBM)] * 3,
        out_specs=pl.BlockSpec(memory_space=pltpu.HBM),
        scratch_shapes=[
            pltpu.VMEM(tokens.shape, tokens.dtype),
            pltpu.VMEM(scale.shape, scale.dtype),
            pltpu.VMEM(names.shape, names.dtype),
            pltpu.VMEM((rows * 8, wide), BF),
            pltpu.SemaphoreType.DMA((3,)),
            pltpu.SemaphoreType.DMA((len(pieces_of(groups, width)),)),
        ],
        compiler_params=pltpu.CompilerParams(vmem_limit_bytes=40 << 20),
    )(*(pltpu.with_memory_space_constraint(x, pltpu.HBM) for x in (tokens, scale, names)))


def table_kernel(chunks, names_ref, weight_ref, *out_refs):
    names = names_ref[...]
    held = ranks(names)
    rows = held.shape[0]
    expert = lax.broadcasted_iota(jnp.int32, (rows, rows), 0)
    weight = jnp.zeros((rows, rows), F32)
    for k in range(names.shape[0]):
        weight = weight + jnp.where(names[k : k + 1, :] == expert, weight_ref[k : k + 1, :], 0.0)
    held, weight = eightfold(held), eightfold(weight)
    at = 0
    for groups in chunks:
        for first, size in groups:
            for c in range(8 // size):
                match = held == wanted(rows, first, size, c)
                own = jnp.where(match, weight, 0.0).reshape(-1, rows).T
                high = own.astype(BF)
                low = (own - high.astype(F32)).astype(BF)
                out_refs[at][2 * c * rows : (2 * c + 1) * rows, :] = high
                out_refs[at][(2 * c + 1) * rows : (2 * c + 2) * rows, :] = low
            at += 1


def tables(chunks, names, weight):
    rows = names.shape[1]
    return pl.pallas_call(
        functools.partial(table_kernel, chunks),
        out_shape=[
            jax.ShapeDtypeStruct((2 * (8 // size) * rows, 8 * rows), BF)
            for groups in chunks
            for _, size in groups
        ],
        in_specs=[pl.BlockSpec(memory_space=pltpu.VMEM)] * 2,
        out_specs=[pl.BlockSpec(memory_space=pltpu.VMEM)] * sum(len(g) for g in chunks),
        compiler_params=pltpu.CompilerParams(vmem_limit_bytes=40 << 20),
    )(names, weight)


def dequantize_kernel(gate_ref, up_ref, down_ref, gs_ref, us_ref, ds_ref, g_ref, u_ref, d_ref):
    for weight_ref, scale_ref, out_ref in (
        (gate_ref, gs_ref, g_ref),
        (up_ref, us_ref, u_ref),
        (down_ref, ds_ref, d_ref),
    ):
        for k in range(weight_ref.shape[0] // BLOCK):
            part = slice(k * BLOCK, (k + 1) * BLOCK)
            out_ref[part, :] = (weight_ref[part, :].astype(F32) * scale_ref[k]).astype(BF)


def dequantize(gate, up, down, gate_scale, up_scale, down_scale):
    width, hidden = gate.shape
    steps = 7
    tall, wide = width // steps, width // steps
    across = lambda scale: jnp.repeat(scale, BLOCK, axis=1)[:, None, :]
    row_spec = pl.BlockSpec((tall, hidden), lambda i: (i, 0))
    col_spec = pl.BlockSpec((hidden, wide), lambda i: (0, i))
    row_scale = pl.BlockSpec((tall // BLOCK, 1, hidden), lambda i: (i, 0, 0))
    col_scale = pl.BlockSpec((hidden // BLOCK, 1, wide), lambda i: (0, 0, i))
    return pl.pallas_call(
        dequantize_kernel,
        grid=(steps,),
        out_shape=[jax.ShapeDtypeStruct(w.shape, BF) for w in (gate, up, down)],
        in_specs=[row_spec, row_spec, col_spec, row_scale, row_scale, col_scale],
        out_specs=[row_spec, row_spec, col_spec],
        compiler_params=pltpu.CompilerParams(vmem_limit_bytes=32 << 20),
    )(gate, up, down, across(gate_scale), across(up_scale), across(down_scale))


def expert_kernel(groups, upper, recv_ref, gate_ref, up_ref, *rest):
    down_refs, (out_ref, x_ref, h_ref, o_ref) = rest[:PART], rest[PART:]
    width = x_ref.shape[1]
    blocks = recv_ref.shape[0] // 256
    tile = gate_ref.shape[1]
    i = pl.program_id(0)

    @pl.when(i == 0)
    def _():
        row = 0
        start = 0
        for _, size in groups:
            cuts = 8 // size
            piece = width // cuts
            tall = 32 * size
            for b in range(blocks):
                block = recv_ref[b * 256 : (b + 1) * 256, start : start + piece]
                if cuts > 1:
                    block = jnp.dot(turn(size, False), block, preferred_element_type=F32)
                    block = block.astype(BF)
                for c in range(cuts):
                    x_ref[row : row + tall, c * piece : (c + 1) * piece] = block[
                        c * tall : (c + 1) * tall
                    ]
                row += tall
            start += piece

    @pl.when(i < upper)
    def _():
        x = x_ref[...]
        gate = jnp.dot(x, gate_ref[...], preferred_element_type=F32)
        up = jnp.dot(x, up_ref[...], preferred_element_type=F32)
        hidden = gate / (1.0 + jnp.exp(-gate)) * up
        h_ref[:, pl.ds(pl.multiple_of(i * tile, tile), tile)] = hidden.astype(BF)

    @pl.when(i >= upper)
    def _():
        down = jnp.concatenate([ref[...] for ref in down_refs], axis=1)
        o_ref[...] = jnp.dot(h_ref[...], down, preferred_element_type=F32).astype(BF)
        row = 0
        start = 0
        for _, size in groups:
            cuts = 8 // size
            lanes = PART * BLOCK // cuts
            tall = 32 * size
            for b in range(blocks):
                block = jnp.concatenate(
                    [
                        o_ref[row : row + tall, c * lanes : (c + 1) * lanes]
                        for c in range(cuts)
                    ],
                    axis=0,
                )
                if cuts > 1:
                    block = jnp.dot(turn(size, True), block, preferred_element_type=F32)
                    block = block.astype(BF)
                out_ref[b * 256 : (b + 1) * 256, start : start + lanes] = block
                row += tall
            start += lanes


def expert(groups, recv, gate, up, down):
    width, hidden = gate.shape
    tile = 256
    upper = hidden // tile
    steps = width // (PART * BLOCK)
    rows = sum(size for _, size in groups) * recv.shape[0] // 8
    lanes = sum(PART * BLOCK * size // 8 for _, size in groups)
    first_spec = pl.BlockSpec((width, tile), lambda i: (0, jnp.minimum(i, upper - 1)))
    down_spec = lambda q: pl.BlockSpec(
        (hidden, BLOCK), lambda i: (0, q * steps + jnp.maximum(i - upper, 0))
    )
    return pl.pallas_call(
        functools.partial(expert_kernel, groups, upper),
        grid=(upper + steps,),
        out_shape=jax.ShapeDtypeStruct((recv.shape[0], lanes * steps), BF),
        in_specs=[
            pl.BlockSpec(recv.shape, lambda i: (0, 0), pipeline_mode=pl.Buffered(1)),
            first_spec,
            first_spec,
        ]
        + [down_spec(q) for q in range(PART)],
        out_specs=pl.BlockSpec((recv.shape[0], lanes), lambda i: (0, jnp.maximum(i - upper, 0))),
        scratch_shapes=[
            pltpu.VMEM((rows, width), BF),
            pltpu.VMEM((rows, hidden), BF),
            pltpu.VMEM((rows, PART * BLOCK), BF),
        ],
        compiler_params=pltpu.CompilerParams(vmem_limit_bytes=52 << 20),
    )(recv, gate, up, *([down] * PART))


def merge_kernel(groups, recv_ref, *rest):
    tables_, out_ref = rest[:-1], rest[-1]
    tokens, width = out_ref.shape
    quarter = width // PART
    t = pl.program_id(0)
    sums = [jnp.zeros((tokens, BLOCK), F32) for _ in range(PART)]
    start = 0
    for (_, size), table_ref in zip(groups, tables_):
        cuts = 8 // size
        lanes = PART * BLOCK // cuts
        got = jnp.dot(
            table_ref[...], recv_ref[:, start : start + lanes], preferred_element_type=F32
        )
        start += lanes
        for c in range(cuts):
            both = got[2 * c * tokens : (2 * c + 1) * tokens] + got[
                (2 * c + 1) * tokens : (2 * c + 2) * tokens
            ]
            for p in range(lanes // BLOCK):
                q = c * (PART // cuts) + p
                sums[q] = sums[q] + both[:, p * BLOCK : (p + 1) * BLOCK]
    for q in range(PART):
        at = pl.ds(pl.multiple_of(q * quarter + t * BLOCK, BLOCK), BLOCK)
        out_ref[:, at] = sums[q]


def merge(groups, recv, tables_):
    steps = 7
    lanes = recv.shape[1] // steps
    tokens = recv.shape[0] // 8
    width = steps * PART * BLOCK
    whole = lambda shape: pl.BlockSpec(shape, lambda t: (0, 0), pipeline_mode=pl.Buffered(1))
    return pl.pallas_call(
        functools.partial(merge_kernel, groups),
        grid=(steps,),
        out_shape=jax.ShapeDtypeStruct((tokens, width), F32),
        in_specs=[pl.BlockSpec((recv.shape[0], lanes), lambda t: (0, t))]
        + [whole(table.shape) for table in tables_],
        out_specs=pl.BlockSpec((tokens, width), lambda t: (0, 0)),
        compiler_params=pltpu.CompilerParams(vmem_limit_bytes=32 << 20),
    )(recv, *tables_)


def finish_kernel(groups, spans, table_refs, before_ref, recv_hbm, out_hbm, *scratch):
    recv_ref, out_ref, in_sems, out_sems = scratch
    tokens, width = out_ref.shape
    quarter = width // PART
    lanes = recv_ref.shape[1] * PART * BLOCK // width
    arrivals = []
    for n, (low, high) in enumerate(spans):
        part = slice(low * lanes, high * lanes)
        arrivals.append(
            pltpu.make_async_copy(recv_hbm.at[:, part], recv_ref.at[:, part], in_sems.at[n])
        )
        arrivals[-1].start()
    departures = []
    for n, (low, high) in enumerate(spans):
        arrivals[n].wait()
        start = 0
        for (_, size), table_ref in zip(groups, table_refs):
            cuts = 8 // size
            wide = PART * BLOCK // cuts
            got = jnp.concatenate(
                [
                    recv_ref[:, t * lanes + start : t * lanes + start + wide]
                    for t in range(low, high)
                ],
                axis=1,
            )
            got = jnp.dot(table_ref[...], got, preferred_element_type=F32)
            for c in range(cuts):
                first = got[2 * c * tokens : (2 * c + 1) * tokens]
                both = first + got[(2 * c + 1) * tokens : (2 * c + 2) * tokens]
                for t in range(low, high):
                    for p in range(wide // BLOCK):
                        q = c * (PART // cuts) + p
                        part = slice(q * quarter + t * BLOCK, q * quarter + (t + 1) * BLOCK)
                        lane = (t - low) * wide + p * BLOCK
                        own = both[:, lane : lane + BLOCK] + before_ref[:, part]
                        out_ref[:, part] = own.astype(out_ref.dtype)
            start += wide
        for q in range(PART):
            part = slice(q * quarter + low * BLOCK, q * quarter + high * BLOCK)
            copy = pltpu.make_async_copy(
                out_ref.at[:, part], out_hbm.at[:, part], out_sems.at[n * PART + q]
            )
            copy.start()
            departures.append(copy)
    for copy in departures:
        copy.wait()


def finish(groups, recv, tables_, before):
    tokens, width = before.shape
    assert len(groups) == 1
    spans = ((0, 3), (3, 7))

    def kernel(*refs):
        finish_kernel(groups, spans, refs[:1], *refs[1:])

    return pl.pallas_call(
        kernel,
        out_shape=pltpu.HBM((tokens, width), BF),
        in_specs=[pl.BlockSpec(memory_space=pltpu.VMEM)] * 2
        + [pl.BlockSpec(memory_space=pltpu.HBM)],
        out_specs=pl.BlockSpec(memory_space=pltpu.HBM),
        scratch_shapes=[
            pltpu.VMEM(recv.shape, BF),
            pltpu.VMEM((tokens, width), BF),
            pltpu.SemaphoreType.DMA((len(spans),)),
            pltpu.SemaphoreType.DMA((len(spans) * PART,)),
        ],
        compiler_params=pltpu.CompilerParams(vmem_limit_bytes=32 << 20),
    )(*tables_, before, recv)


def exchange(block):
    rows, wide = block.shape
    block = lax.all_to_all(
        block.reshape(rows // 8, 8, wide), AXES, split_axis=0, concat_axis=0, tiled=True
    )
    return block.reshape(rows, wide)


def local(
    tokens, act_scale, routes, combine, w_gate, gate_scale, w_up, up_scale, w_down, down_scale
):
    route_count = routes.shape[1]
    experts = lax.axis_size("node") * lax.axis_size("local")
    capacity = 5 * tokens.shape[0] * route_count // (4 * experts)
    one, two = groups_of(0, FIRST), groups_of(FIRST, capacity)
    names, scale = routes.T, act_scale.T
    send_one = pack(one, tokens, scale, names)
    recv_one = exchange(send_one)
    send_two = pack(two, tokens, scale, names)
    weights = dequantize(w_gate[0], w_up[0], w_down[0], gate_scale[0], up_scale[0], down_scale[0])
    found = tables((one, two), names, combine.T)
    recv_two = exchange(send_two)
    done_one = expert(one, recv_one, *weights)
    back_one = exchange(done_one)
    done_two = expert(two, recv_two, *weights)
    back_two = exchange(done_two)
    total = merge(one, back_one, found[: len(one)])
    return finish(two, back_two, found[len(one) :], total)


def solution(mesh):
    placed = (P(AXES, None),) * 4 + (P(AXES, None, None),) * 6
    return jax.shard_map(
        local, mesh=mesh, in_specs=placed, out_specs=P(AXES, None), check_vma=False
    )
```

```python
import functools

import jax
import jax.numpy as jnp
from jax import lax
from jax.experimental import pallas as pl
from jax.experimental.pallas import tpu as pltpu
from jax.sharding import PartitionSpec as P


AXES = ("node", "local")
BLOCK = 128
PART = 4
FIRST = 6
BF = jnp.bfloat16
F32 = jnp.float32


def groups_of(first, last):
    groups = []
    for size in (8, 4, 2):
        while last - first >= size:
            groups.append((first, size))
            first += size
    return groups


def ranks(names):
    count, rows = names.shape
    expert = lax.broadcasted_iota(jnp.int32, (rows, rows), 0)
    named = jnp.zeros((rows, rows), F32)
    for k in range(count):
        named = named + jnp.where(names[k : k + 1, :] == expert, 1.0, 0.0)
    later = lax.broadcasted_iota(jnp.int32, (rows, rows), 0) < lax.broadcasted_iota(
        jnp.int32, (rows, rows), 1
    )
    before = jnp.dot(
        named.astype(BF), jnp.where(later, 1.0, 0.0).astype(BF), preferred_element_type=F32
    )
    return jnp.where(named > 0.5, before, -1.0)


def eightfold(table):
    rows, cols = table.shape
    return jnp.broadcast_to(table[:, None, :], (rows, 8, cols))


def wanted(cols, first, size, cut):
    row = lax.broadcasted_iota(jnp.int32, (1, 8, cols), 1)
    slot = (row & (size - 1)) + first
    return jnp.where(row >> (size.bit_length() - 1) == cut, slot, -2).astype(F32)


def turn(size, back):
    shape = (256, 256)
    out = lax.broadcasted_iota(jnp.int32, shape, 1 if back else 0)
    held = lax.broadcasted_iota(jnp.int32, shape, 0 if back else 1)
    low = size.bit_length() - 1
    piece = out >> (5 + low)
    source = (out >> low) & 31
    slot = out & (size - 1)
    return jnp.where(held == source * 8 + piece * size + slot, 1.0, 0.0).astype(BF)


def pack_kernel(groups, parts, tokens_hbm, scale_hbm, names_hbm, out_hbm, *scratch):
    tokens_ref, scale_ref, names_ref, out_ref, in_sems, out_sems = scratch
    arrivals = [
        pltpu.make_async_copy(source, target, in_sems.at[n])
        for n, (source, target) in enumerate(
            (
                (names_hbm, names_ref),
                (scale_hbm, scale_ref),
                (tokens_hbm, tokens_ref),
            )
        )
    ]
    for copy in arrivals:
        copy.start()
    rows, width = tokens_ref.shape
    blocks = scale_ref.shape[0]
    arrivals[0].wait()
    held = eightfold(ranks(names_ref[...]))
    lane = lax.broadcasted_iota(jnp.int32, (blocks, width), 1)
    spread = jnp.where(
        (lane >> 7) == lax.broadcasted_iota(jnp.int32, (blocks, width), 0), 1.0, 0.0
    ).astype(BF)
    arrivals[1].wait()
    scale = lax.dot_general(
        scale_ref[...].astype(BF), spread, (((0,), (0,)), ((), ())), preferred_element_type=F32
    )
    arrivals[2].wait()
    inputs = tokens_ref[...] * scale.astype(BF)
    departures = []
    tall = rows // parts
    for part_at in range(parts):
        held_part = held[part_at * tall : (part_at + 1) * tall]
        below = slice(part_at * tall * 8, (part_at + 1) * tall * 8)
        begin = 0
        for first, size in groups:
            cuts = 8 // size
            piece = width // cuts
            table = jnp.concatenate(
                [
                    jnp.where(held_part == wanted(rows, first, size, c), 1.0, 0.0)
                    .astype(BF)
                    .reshape(-1, rows)
                    for c in range(cuts)
                ],
                axis=1,
            )
            for start in range(0, piece, 512):
                lanes = min(512, piece - start)
                stacked = jnp.concatenate(
                    [inputs[:, c * piece + start : c * piece + start + lanes] for c in range(cuts)],
                    axis=0,
                )
                out_ref[below, begin : begin + lanes] = jnp.dot(
                    table, stacked, preferred_element_type=F32
                ).astype(BF)
                begin += lanes
        copy = pltpu.make_async_copy(
            out_ref.at[below, :], out_hbm.at[below, :], out_sems.at[part_at]
        )
        copy.start()
        departures.append(copy)
    for copy in departures:
        copy.wait()


def pack(groups, tokens, scale, names):
    rows, width = tokens.shape
    parts = 8
    wide = sum(width * size // 8 for _, size in groups)
    return pl.pallas_call(
        functools.partial(pack_kernel, groups, parts),
        out_shape=pltpu.HBM((rows * 8, wide), BF),
        in_specs=[pl.BlockSpec(memory_space=pltpu.HBM)] * 3,
        out_specs=pl.BlockSpec(memory_space=pltpu.HBM),
        scratch_shapes=[
            pltpu.VMEM(tokens.shape, tokens.dtype),
            pltpu.VMEM(scale.shape, scale.dtype),
            pltpu.VMEM(names.shape, names.dtype),
            pltpu.VMEM((rows * 8, wide), BF),
            pltpu.SemaphoreType.DMA((3,)),
            pltpu.SemaphoreType.DMA((parts,)),
        ],
        compiler_params=pltpu.CompilerParams(vmem_limit_bytes=40 << 20),
    )(*(pltpu.with_memory_space_constraint(x, pltpu.HBM) for x in (tokens, scale, names)))


def table_kernel(chunks, names_ref, weight_ref, *out_refs):
    names = names_ref[...]
    held = ranks(names)
    rows = held.shape[0]
    expert = lax.broadcasted_iota(jnp.int32, (rows, rows), 0)
    weight = jnp.zeros((rows, rows), F32)
    for k in range(names.shape[0]):
        weight = weight + jnp.where(names[k : k + 1, :] == expert, weight_ref[k : k + 1, :], 0.0)
    held, weight = eightfold(held), eightfold(weight)
    at = 0
    for groups in chunks:
        for first, size in groups:
            for c in range(8 // size):
                match = held == wanted(rows, first, size, c)
                own = jnp.where(match, weight, 0.0).reshape(-1, rows).T
                high = own.astype(BF)
                low = (own - high.astype(F32)).astype(BF)
                out_refs[at][2 * c * rows : (2 * c + 1) * rows, :] = high
                out_refs[at][(2 * c + 1) * rows : (2 * c + 2) * rows, :] = low
            at += 1


def tables(chunks, names, weight):
    rows = names.shape[1]
    return pl.pallas_call(
        functools.partial(table_kernel, chunks),
        out_shape=[
            jax.ShapeDtypeStruct((2 * (8 // size) * rows, 8 * rows), BF)
            for groups in chunks
            for _, size in groups
        ],
        in_specs=[pl.BlockSpec(memory_space=pltpu.VMEM)] * 2,
        out_specs=[pl.BlockSpec(memory_space=pltpu.VMEM)] * sum(len(g) for g in chunks),
        compiler_params=pltpu.CompilerParams(vmem_limit_bytes=40 << 20),
    )(names, weight)


def dequantize_kernel(gate_ref, up_ref, down_ref, gs_ref, us_ref, ds_ref, g_ref, u_ref, d_ref):
    for weight_ref, scale_ref, out_ref in (
        (gate_ref, gs_ref, g_ref),
        (up_ref, us_ref, u_ref),
        (down_ref, ds_ref, d_ref),
    ):
        for k in range(weight_ref.shape[0] // BLOCK):
            part = slice(k * BLOCK, (k + 1) * BLOCK)
            out_ref[part, :] = (weight_ref[part, :].astype(F32) * scale_ref[k]).astype(BF)


def dequantize(gate, up, down, gate_scale, up_scale, down_scale):
    width, hidden = gate.shape
    steps = 7
    tall, wide = width // steps, width // steps
    across = lambda scale: jnp.repeat(scale, BLOCK, axis=1)[:, None, :]
    row_spec = pl.BlockSpec((tall, hidden), lambda i: (i, 0))
    col_spec = pl.BlockSpec((hidden, wide), lambda i: (0, i))
    row_scale = pl.BlockSpec((tall // BLOCK, 1, hidden), lambda i: (i, 0, 0))
    col_scale = pl.BlockSpec((hidden // BLOCK, 1, wide), lambda i: (0, 0, i))
    return pl.pallas_call(
        dequantize_kernel,
        grid=(steps,),
        out_shape=[jax.ShapeDtypeStruct(w.shape, BF) for w in (gate, up, down)],
        in_specs=[row_spec, row_spec, col_spec, row_scale, row_scale, col_scale],
        out_specs=[row_spec, row_spec, col_spec],
        compiler_params=pltpu.CompilerParams(vmem_limit_bytes=32 << 20),
    )(gate, up, down, across(gate_scale), across(up_scale), across(down_scale))


def expert_kernel(groups, upper, recv_ref, gate_ref, up_ref, *rest):
    down_refs, (out_ref, x_ref, h_ref, o_ref) = rest[:PART], rest[PART:]
    width = x_ref.shape[1]
    blocks = recv_ref.shape[0] // 256
    tile = gate_ref.shape[1]
    i = pl.program_id(0)

    @pl.when(i == 0)
    def _():
        row = 0
        start = 0
        for _, size in groups:
            cuts = 8 // size
            piece = width // cuts
            tall = 32 * size
            for b in range(blocks):
                block = recv_ref[b * 256 : (b + 1) * 256, start : start + piece]
                if cuts > 1:
                    block = jnp.dot(turn(size, False), block, preferred_element_type=F32)
                    block = block.astype(BF)
                for c in range(cuts):
                    x_ref[row : row + tall, c * piece : (c + 1) * piece] = block[
                        c * tall : (c + 1) * tall
                    ]
                row += tall
            start += piece

    @pl.when(i < upper)
    def _():
        x = x_ref[...]
        gate = jnp.dot(x, gate_ref[...], preferred_element_type=F32)
        up = jnp.dot(x, up_ref[...], preferred_element_type=F32)
        hidden = gate / (1.0 + jnp.exp(-gate)) * up
        h_ref[:, pl.ds(pl.multiple_of(i * tile, tile), tile)] = hidden.astype(BF)

    @pl.when(i >= upper)
    def _():
        down = jnp.concatenate([ref[...] for ref in down_refs], axis=1)
        o_ref[...] = jnp.dot(h_ref[...], down, preferred_element_type=F32).astype(BF)
        row = 0
        start = 0
        for _, size in groups:
            cuts = 8 // size
            lanes = PART * BLOCK // cuts
            tall = 32 * size
            for b in range(blocks):
                block = jnp.concatenate(
                    [
                        o_ref[row : row + tall, c * lanes : (c + 1) * lanes]
                        for c in range(cuts)
                    ],
                    axis=0,
                )
                if cuts > 1:
                    block = jnp.dot(turn(size, True), block, preferred_element_type=F32)
                    block = block.astype(BF)
                out_ref[b * 256 : (b + 1) * 256, start : start + lanes] = block
                row += tall
            start += lanes


def expert(groups, recv, gate, up, down):
    width, hidden = gate.shape
    tile = 256
    upper = hidden // tile
    steps = width // (PART * BLOCK)
    rows = sum(size for _, size in groups) * recv.shape[0] // 8
    lanes = sum(PART * BLOCK * size // 8 for _, size in groups)
    first_spec = pl.BlockSpec((width, tile), lambda i: (0, jnp.minimum(i, upper - 1)))
    down_spec = lambda q: pl.BlockSpec(
        (hidden, BLOCK), lambda i: (0, q * steps + jnp.maximum(i - upper, 0))
    )
    return pl.pallas_call(
        functools.partial(expert_kernel, groups, upper),
        grid=(upper + steps,),
        out_shape=jax.ShapeDtypeStruct((recv.shape[0], lanes * steps), BF),
        in_specs=[
            pl.BlockSpec(recv.shape, lambda i: (0, 0), pipeline_mode=pl.Buffered(1)),
            first_spec,
            first_spec,
        ]
        + [down_spec(q) for q in range(PART)],
        out_specs=pl.BlockSpec((recv.shape[0], lanes), lambda i: (0, jnp.maximum(i - upper, 0))),
        scratch_shapes=[
            pltpu.VMEM((rows, width), BF),
            pltpu.VMEM((rows, hidden), BF),
            pltpu.VMEM((rows, PART * BLOCK), BF),
        ],
        compiler_params=pltpu.CompilerParams(vmem_limit_bytes=52 << 20),
    )(recv, gate, up, *([down] * PART))


def merge_kernel(groups, recv_ref, *rest):
    tables_, out_ref = rest[:-1], rest[-1]
    tokens, width = out_ref.shape
    quarter = width // PART
    t = pl.program_id(0)
    sums = [jnp.zeros((tokens, BLOCK), F32) for _ in range(PART)]
    start = 0
    for (_, size), table_ref in zip(groups, tables_):
        cuts = 8 // size
        lanes = PART * BLOCK // cuts
        got = jnp.dot(
            table_ref[...], recv_ref[:, start : start + lanes], preferred_element_type=F32
        )
        start += lanes
        for c in range(cuts):
            both = got[2 * c * tokens : (2 * c + 1) * tokens] + got[
                (2 * c + 1) * tokens : (2 * c + 2) * tokens
            ]
            for p in range(lanes // BLOCK):
                q = c * (PART // cuts) + p
                sums[q] = sums[q] + both[:, p * BLOCK : (p + 1) * BLOCK]
    for q in range(PART):
        at = pl.ds(pl.multiple_of(q * quarter + t * BLOCK, BLOCK), BLOCK)
        out_ref[:, at] = sums[q]


def merge(groups, recv, tables_):
    steps = 7
    lanes = recv.shape[1] // steps
    tokens = recv.shape[0] // 8
    width = steps * PART * BLOCK
    whole = lambda shape: pl.BlockSpec(shape, lambda t: (0, 0), pipeline_mode=pl.Buffered(1))
    return pl.pallas_call(
        functools.partial(merge_kernel, groups),
        grid=(steps,),
        out_shape=jax.ShapeDtypeStruct((tokens, width), F32),
        in_specs=[pl.BlockSpec((recv.shape[0], lanes), lambda t: (0, t))]
        + [whole(table.shape) for table in tables_],
        out_specs=pl.BlockSpec((tokens, width), lambda t: (0, 0)),
        compiler_params=pltpu.CompilerParams(vmem_limit_bytes=32 << 20),
    )(recv, *tables_)


def finish_kernel(groups, spans, table_refs, before_ref, recv_hbm, out_hbm, *scratch):
    recv_ref, out_ref, in_sems, out_sems = scratch
    tokens, width = out_ref.shape
    quarter = width // PART
    lanes = recv_ref.shape[1] * PART * BLOCK // width
    arrivals = []
    for n, (low, high) in enumerate(spans):
        part = slice(low * lanes, high * lanes)
        arrivals.append(
            pltpu.make_async_copy(recv_hbm.at[:, part], recv_ref.at[:, part], in_sems.at[n])
        )
        arrivals[-1].start()
    departures = []
    for n, (low, high) in enumerate(spans):
        arrivals[n].wait()
        start = 0
        for (_, size), table_ref in zip(groups, table_refs):
            cuts = 8 // size
            wide = PART * BLOCK // cuts
            for c in range(cuts):
                table = table_ref[2 * c * tokens : 2 * (c + 1) * tokens, :]
                got = jnp.concatenate(
                    [
                        recv_ref[:, t * lanes + start : t * lanes + start + wide]
                        for t in range(low, high)
                    ],
                    axis=1,
                )
                got = jnp.dot(table, got, preferred_element_type=F32)
                both = got[:tokens] + got[tokens:]
                for t in range(low, high):
                    for p in range(wide // BLOCK):
                        q = c * (PART // cuts) + p
                        part = slice(q * quarter + t * BLOCK, q * quarter + (t + 1) * BLOCK)
                        lane = (t - low) * wide + p * BLOCK
                        own = both[:, lane : lane + BLOCK] + before_ref[:, part]
                        out_ref[:, part] = own.astype(out_ref.dtype)
            start += wide
        for q in range(PART):
            part = slice(q * quarter + low * BLOCK, q * quarter + high * BLOCK)
            copy = pltpu.make_async_copy(
                out_ref.at[:, part], out_hbm.at[:, part], out_sems.at[n * PART + q]
            )
            copy.start()
            departures.append(copy)
    for copy in departures:
        copy.wait()


def finish(groups, recv, tables_, before):
    tokens, width = before.shape
    assert len(groups) == 1
    spans = ((0, 1), (1, 3), (3, 7))

    def kernel(*refs):
        finish_kernel(groups, spans, refs[:1], *refs[1:])

    return pl.pallas_call(
        kernel,
        out_shape=pltpu.HBM((tokens, width), BF),
        in_specs=[pl.BlockSpec(memory_space=pltpu.VMEM)] * 2
        + [pl.BlockSpec(memory_space=pltpu.HBM)],
        out_specs=pl.BlockSpec(memory_space=pltpu.HBM),
        scratch_shapes=[
            pltpu.VMEM(recv.shape, BF),
            pltpu.VMEM((tokens, width), BF),
            pltpu.SemaphoreType.DMA((len(spans),)),
            pltpu.SemaphoreType.DMA((len(spans) * PART,)),
        ],
        compiler_params=pltpu.CompilerParams(vmem_limit_bytes=32 << 20),
    )(*tables_, before, recv)


def exchange(block):
    rows, wide = block.shape
    block = lax.all_to_all(
        block.reshape(rows // 8, 8, wide), AXES, split_axis=0, concat_axis=0, tiled=True
    )
    return block.reshape(rows, wide)


def local(
    tokens, act_scale, routes, combine, w_gate, gate_scale, w_up, up_scale, w_down, down_scale
):
    route_count = routes.shape[1]
    experts = lax.axis_size("node") * lax.axis_size("local")
    capacity = 5 * tokens.shape[0] * route_count // (4 * experts)
    one, two = groups_of(0, FIRST), groups_of(FIRST, capacity)
    names, scale = routes.T, act_scale.T
    send_one = pack(one, tokens, scale, names)
    recv_one = exchange(send_one)
    send_two = pack(two, tokens, scale, names)
    weights = dequantize(w_gate[0], w_up[0], w_down[0], gate_scale[0], up_scale[0], down_scale[0])
    found = tables((one, two), names, combine.T)
    recv_two = exchange(send_two)
    done_one = expert(one, recv_one, *weights)
    back_one = exchange(done_one)
    done_two = expert(two, recv_two, *weights)
    back_two = exchange(done_two)
    total = merge(one, back_one, found[: len(one)])
    return finish(two, back_two, found[len(one) :], total)


def solution(mesh):
    placed = (P(AXES, None),) * 4 + (P(AXES, None, None),) * 6
    return jax.shard_map(
        local, mesh=mesh, in_specs=placed, out_specs=P(AXES, None), check_vma=False
    )
```
